128 devices in a mesh: seq: 32 (over z, x, core), head: 4 (over y).
Axes of the slice: x: 4, y: 4, z: 4, core: 2. Of those that a mesh axis runs over, the one named last changes fastest.
Arguments:
- prompt_q: bfloat16 [32768, 2048], P('seq', 'head'), may hold values from -6 to 6
- prompt_k: bfloat16 [32768, 2048], P('seq', 'head'), may hold values from -6 to 6
- prompt_v: bfloat16 [32768, 2048], P('seq', 'head'), may hold values from -6 to 6
- prompt_grad: bfloat16 [32768, 2048], P('seq', 'head'), may hold values from -6 to 6
- cand_q: bfloat16 [16384, 2048], P('seq', 'head'), may hold values from -6 to 6
- cand_k: bfloat16 [16384, 2048], P('seq', 'head'), may hold values from -6 to 6
- cand_v: bfloat16 [16384, 2048], P('seq', 'head'), may hold values from -6 to 6
- readout: float32 [2048], P('head'), may hold values from -0.24 to 0.24
- prompt_ends: int32 [32], replicated, may hold values from 1 to 32768, as said below
- cand_lengths: int32 [32, 2], P('seq'), may hold values from 1 to 384, 512 in all within a row
- cand_prompt: int32 [64], replicated, may hold values from 0 to 31
- cand_ranks: int32 [64], replicated, may hold values from 0 to 3
Outputs:
- prompt_dq: bfloat16 [32768, 2048], P('seq', 'head')
- prompt_dk: bfloat16 [32768, 2048], P('seq', 'head')
- prompt_dv: bfloat16 [32768, 2048], P('seq', 'head')
- cand_dq: bfloat16 [16384, 2048], P('seq', 'head')
- cand_dk: bfloat16 [16384, 2048], P('seq', 'head')
- cand_dv: bfloat16 [16384, 2048], P('seq', 'head')
- list_loss: float32 [], replicated
The draws below stay inside these ranges and needn't reach their ends.
Inputs may be any that keep to these rules, and one draw needn't show every extreme that they name: `prompt_ends`: strictly increasing; the last equals 32768; at most 2 ends lie in each range (d * 1024, (d + 1) * 1024], and in some range exactly 2. `cand_lengths`: each row sums to 512, and no entry exceeds 384.
All inputs are finite; a program needn't handle non-finite values.
Results may differ from the reference program's by a relative error of at most 0.0062.
Values may be sent and summed in bfloat16 or wider, within the bound.
A program may use at most 128 MiB of HBM per device.

```python
import math
import jax
import jax.numpy as jnp
import numpy as np
from jax import lax

HEADS = 16
E = 128
P_DEV = 1024
C_DEV = 512
NC_DEV = 2
ENDS = 2
PROMPTS = 32
TOTAL = 32768
CTOTAL = 16384
NCAND = 64
CMAX = 384
N_SEQ = 32


def draw_prompt_ends(key, part):
    device_count = PROMPTS
    slot_total = device_count * ENDS
    slot_span = P_DEV // ENDS
    early_blocks = device_count // 2 + 1
    key_order, key_device, key_offset = jax.random.split(jax.random.fold_in(key, 7), 3)
    slot_order = jax.random.permutation(key_order, slot_total).astype(jnp.int32)
    chosen = jax.random.randint(key_device, (), 0, early_blocks).astype(jnp.int32)
    slot_ids = jnp.arange(slot_total, dtype=jnp.int32)
    device_of = slot_ids // ENDS
    slot_of = slot_ids % ENDS
    forced_full = device_of == chosen
    forced_last = slot_ids == slot_total - 1
    eligible = device_of < early_blocks
    normal_rank = jnp.where(eligible, slot_order, slot_total + slot_ids)
    priority = jnp.where(jnp.logical_or(forced_full, forced_last), -1 - slot_ids, normal_rank)
    ranked = jnp.argsort(priority, stable=True)
    selected = jnp.zeros((slot_total,), jnp.int32).at[ranked[:device_count]].set(1)
    offsets = slot_of * slot_span + jax.random.randint(key_offset, (slot_total,), 1, slot_span + 1).astype(jnp.int32)
    offsets = jnp.where(forced_last, P_DEV, offsets)
    positions = device_of * P_DEV + offsets
    marked = jnp.where(selected > 0, positions, slot_total * P_DEV + 1)
    return jnp.sort(marked)[:device_count].astype(jnp.int32)


def place_ends(result, stream_key, least, high):
    longest = result.shape.index(max(result.shape))
    spots = []
    for shift in (0, 1):
        where = [jax.random.randint(jax.random.fold_in(stream_key, axis), (), 0, length) for axis, length in enumerate(result.shape)]
        where[longest] = (where[longest] + shift) % result.shape[longest]
        spots.append(tuple(where))
    return result.at[spots[0]].set(least).at[spots[1]].set(high)


def block_levels(own_key, extent, cuts, low, high):
    level = 1.0
    for axis_at, blocks in cuts:
        steps = jax.random.uniform(jax.random.fold_in(jax.random.fold_in(own_key, 6), axis_at), (blocks,), jnp.float32, low / len(cuts), high / len(cuts))
        level = level * jnp.repeat(jnp.exp(steps), extent[axis_at] // blocks).reshape((-1,) + (1,) * (len(extent) - 1 - axis_at))
    return level


def split_up(number_of, total, bound, lean):
    portions = [(1 << 20) // math.isqrt(rank ** lean) + 1 for rank in range(2, number_of + 1)]
    rest, counts = total - bound - (number_of - 1), [1] * (number_of - 1)
    while rest > 0:
        candidates = [i for i in range(number_of - 1) if counts[i] < bound]
        pool, left = sum([portions[i] for i in candidates]), rest
        for i in candidates:
            extra = min(bound - counts[i], max(1, left * portions[i] // pool), rest)
            counts[i] = counts[i] + extra
            rest = rest - extra
    return np.array([bound] + counts)


def uneven_parts(key, count, total, most, skew):
    if count == 2:
        one = jax.random.randint(key, (), max(1, total - most), min(most, total - 1) + 1)
        return jnp.stack([one, total - one])
    sizes = jnp.asarray(split_up(count, total, most, skew), jnp.int32)
    couples = (count - 1) // 2
    donor, receiver = sizes[1:1 + 2 * couples:2], sizes[2:2 + 2 * couples:2]
    room = jnp.minimum(donor - 1, most - receiver)
    shifted = jax.random.randint(jax.random.fold_in(key, 1), (couples,), 0, 1 << 20) % (room + 1)
    sizes = sizes.at[1:1 + 2 * couples:2].set(donor - shifted).at[2:2 + 2 * couples:2].set(receiver + shifted)
    return sizes[jax.random.permutation(jax.random.fold_in(key, 2), count)]


def noise(own_key, dims, width, reach, cuts=(), kind=jnp.bfloat16):
    array = jax.random.normal(own_key, dims, jnp.float32) * width
    if len(cuts) > 0:
        array = block_levels(own_key, dims, cuts, -0.22, 0.18) * array
    return jnp.clip(array, min=-reach, max=reach).astype(kind)


def setup_inputs(seed: int = 0) -> dict:
    key_of = jax.random.split(jax.random.key(seed), 13)
    return {
        "prompt_q": noise(key_of[0], (TOTAL, HEADS * E), 1.0, 6.0, ((0, 32), (1, 4))),
        "prompt_k": noise(key_of[1], (TOTAL, HEADS * E), 1.0, 6.0, ((0, 32), (1, 4))),
        "prompt_v": noise(key_of[2], (TOTAL, HEADS * E), 1.0, 6.0, ((0, 32), (1, 4))),
        "prompt_grad": noise(key_of[3], (TOTAL, HEADS * E), 1.0, 6.0, ((0, 32), (1, 4))),
        "cand_q": noise(key_of[4], (CTOTAL, HEADS * E), 1.0, 6.0, ((0, 32), (1, 4))),
        "cand_k": noise(key_of[5], (CTOTAL, HEADS * E), 1.0, 6.0, ((0, 32), (1, 4))),
        "cand_v": noise(key_of[6], (CTOTAL, HEADS * E), 1.0, 6.0, ((0, 32), (1, 4))),
        "readout": noise(key_of[7], (HEADS * E,), 0.04, 0.24, ((0, 4),), jnp.float32),
        "prompt_ends": draw_prompt_ends(jax.random.fold_in(key_of[12], 71), 0),
        "cand_lengths": jax.vmap(lambda own: uneven_parts(own, NC_DEV, C_DEV, CMAX, 1))(jax.random.split(key_of[9], N_SEQ)).reshape((N_SEQ, NC_DEV)).astype(jnp.int32),
        "cand_prompt": place_ends(jax.random.randint(key_of[10], (NCAND,), 0, PROMPTS), jax.random.fold_in(key_of[10], 1), 0, PROMPTS - 1).astype(jnp.int32),
        "cand_ranks": place_ends(jax.random.randint(key_of[11], (NCAND,), 0, 4), jax.random.fold_in(key_of[11], 1), 0, 3).astype(jnp.int32),
    }


grad_scale = 1048576.0

def product_of(form, left, right):
    return jnp.einsum(form, left.astype(jnp.float32), right.astype(jnp.float32), precision=lax.Precision.HIGHEST)

def pick_value(table, wanted):
    spots = jnp.arange(table.shape[0], dtype=jnp.int32)
    return jnp.sum(jnp.where(spots == wanted, table, 0)).astype(jnp.int32)

def slab_layout(prompt_ends, slab_index, slab_width, slot_count):
    prompt_count = prompt_ends.shape[0]
    slab_start = slab_index * slab_width
    position = slab_start + jnp.arange(slab_width, dtype=jnp.int32)
    segment = lax.optimization_barrier(jnp.sum((prompt_ends[None, :] <= position[:, None]).astype(jnp.int32), axis=1)).astype(jnp.int32)
    begins = jnp.logical_or(slab_index == 0, jnp.any(prompt_ends == slab_start))
    first_seg = segment[0]
    last_seg = segment[slab_width - 1]
    first_end = jnp.sum((prompt_ends <= slab_start).astype(jnp.int32)).astype(jnp.int32)
    slot_pid = first_end + jnp.arange(slot_count, dtype=jnp.int32)
    prompt_ids = jnp.arange(prompt_count, dtype=jnp.int32)
    slot_end = lax.optimization_barrier(jnp.sum(jnp.where(prompt_ids[None, :] == slot_pid[:, None], prompt_ends[None, :], 0), axis=1)).astype(jnp.int32)
    slot_valid = jnp.logical_and(slot_pid < prompt_count, slot_end <= slab_start + slab_width)
    slot_masks = jnp.logical_and(segment[None, :] == slot_pid[:, None], slot_valid[:, None])
    row_masks = jnp.concatenate([slot_masks, (segment == last_seg)[None, :]], axis=0).astype(jnp.float32)
    start_flag = jnp.logical_or(begins, first_seg != last_seg).astype(jnp.float32)
    end_flag = slot_valid[0].astype(jnp.float32)
    cont_right = (pick_value(prompt_ends, last_seg) != slab_start + slab_width).astype(jnp.float32)
    contin = 1.0 - begins.astype(jnp.float32)
    first_mask = (segment == first_seg).astype(jnp.float32)
    from_first = jnp.logical_and(slot_pid == first_seg, slot_valid).astype(jnp.float32)
    return (segment, row_masks, first_mask, contin, from_first, slot_pid, slot_valid, start_flag, end_flag, cont_right)

def cand_layout(lengths, cand_width):
    bounds = jnp.cumsum(lengths).astype(jnp.int32)
    tok_pos = jnp.arange(cand_width, dtype=jnp.int32)
    cand_id = lax.optimization_barrier(jnp.sum((bounds[None, :] <= tok_pos[:, None]).astype(jnp.int32), axis=1)).astype(jnp.int32)
    cand_masks = (cand_id[None, :] == jnp.arange(lengths.shape[0], dtype=jnp.int32)[:, None]).astype(jnp.float32)
    same_cand = jnp.logical_and(cand_id[:, None] == cand_id[None, :], tok_pos[None, :] <= tok_pos[:, None])
    return (cand_masks, same_cand)

def listwise(raw_scores, cand_prompt, cand_ranks, prompt_count):
    squashed = 3.0 * jnp.tanh(raw_scores)
    same_group = (cand_prompt[:, None] == cand_prompt[None, :]).astype(jnp.float32)
    exp_scores = jnp.exp(squashed)
    denoms = lax.optimization_barrier(jnp.sum(same_group * exp_scores[None, :], axis=1))
    rank_weight = jnp.exp(-cand_ranks.astype(jnp.float32))
    targets = rank_weight / lax.optimization_barrier(jnp.sum(same_group * rank_weight[None, :], axis=1))
    list_loss = -jnp.sum(targets * (squashed - jnp.log(denoms))) / prompt_count
    tanh_raw = jnp.tanh(raw_scores)
    raw_grad = grad_scale / prompt_count * (exp_scores / denoms - targets) * 3.0 * (1.0 - tanh_raw * tanh_raw)
    return (list_loss, raw_grad)

def reference(prompt_q, prompt_k, prompt_v, prompt_grad, cand_q, cand_k, cand_v, readout, prompt_ends, cand_lengths, cand_prompt, cand_ranks):
    scaling = 1.0 / math.sqrt(E * P_DEV)
    slab_ids = jnp.arange(N_SEQ, dtype=jnp.int32)
    queries = prompt_q.reshape(N_SEQ, P_DEV, HEADS, E)
    keys_in = prompt_k.reshape(N_SEQ, P_DEV, HEADS, E)
    values_in = prompt_v.reshape(N_SEQ, P_DEV, HEADS, E)
    grads_in = prompt_grad.reshape(N_SEQ, P_DEV, HEADS, E)
    cand_queries = cand_q.reshape(N_SEQ, C_DEV, HEADS, E)
    cand_keys = cand_k.reshape(N_SEQ, C_DEV, HEADS, E)
    cand_values = cand_v.reshape(N_SEQ, C_DEV, HEADS, E)
    readout_heads = readout.reshape(HEADS, E)

    def layout_of(slab_index):
        return slab_layout(prompt_ends, slab_index, P_DEV, ENDS)
    segments, row_masks, first_masks, contins, from_first, slot_pid, slot_valid, start_flags, end_flags, cont_rights = jax.vmap(layout_of)(slab_ids)

    def local_sums(inputs):
        masks_one, keys_blk, values_blk = inputs
        return product_of('mthd,the->mhde', masks_one[:, :, None, None] * keys_blk[None].astype(jnp.float32), values_blk)
    slab_sums = lax.map(local_sums, (row_masks, keys_in, values_in))

    def forward_chain(running, inputs):
        tail_state, start_flag = inputs
        return (tail_state + (1.0 - start_flag) * running, running)
    zero_state = jnp.zeros((HEADS, E, E), jnp.float32)
    unused_state, incoming = lax.scan(forward_chain, zero_state, (slab_sums[:, ENDS], start_flags))
    incoming_first = contins[:, None, None, None] * incoming
    valid_float = slot_valid.astype(jnp.float32)
    end_slots = (slab_sums[:, :ENDS] + from_first[:, :, None, None, None] * incoming_first[:, None]) * valid_float[:, :, None, None, None]
    end_states = end_slots.astype(jnp.bfloat16)
    target_rows = jnp.where(slot_valid, slot_pid, PROMPTS).reshape(-1).astype(jnp.int32)
    by_prompt = jnp.zeros((PROMPTS + 1, HEADS, E, E), jnp.float32).at[target_rows].add(end_states.reshape(-1, HEADS, E, E).astype(jnp.float32))
    cand_states = by_prompt[cand_prompt].astype(jnp.bfloat16).reshape(N_SEQ, NC_DEV, HEADS, E, E)

    def cand_forward(slab_q, slab_k, slab_v, slab_lengths, slab_states):
        cand_masks, same_cand = cand_layout(slab_lengths, C_DEV)
        qk_scores = product_of('thd,shd->hts', slab_q, slab_k)
        attn_weights = jnp.where(same_cand[None], qk_scores, 0.0).astype(jnp.bfloat16)
        masked_queries = cand_masks[:, :, None, None] * slab_q[None].astype(jnp.float32)
        outputs = scaling * (product_of('hts,she->the', attn_weights, slab_v) + product_of('jthd,jhde->the', masked_queries, slab_states))
        return (cand_masks, same_cand, attn_weights, masked_queries, outputs)

    def cand_scores(inputs):
        slab_q, slab_k, slab_v, slab_lengths, slab_states = inputs
        cand_masks, same_cand, attn_weights, masked_queries, outputs = cand_forward(slab_q, slab_k, slab_v, slab_lengths, slab_states)
        token_score = lax.optimization_barrier(jnp.sum(jax.nn.silu(outputs) * readout_heads[None], axis=(1, 2)))
        return lax.optimization_barrier(jnp.sum(cand_masks * token_score[None, :], axis=1)) / slab_lengths.astype(jnp.float32)
    raw_scores = lax.map(cand_scores, (cand_queries, cand_keys, cand_values, cand_lengths, cand_states)).reshape(-1)
    list_loss, raw_grad = listwise(raw_scores, cand_prompt, cand_ranks, PROMPTS)

    def cand_backward(inputs):
        slab_q, slab_k, slab_v, slab_lengths, slab_states, slab_grad = inputs
        cand_masks, same_cand, attn_weights, masked_queries, outputs = cand_forward(slab_q, slab_k, slab_v, slab_lengths, slab_states)
        token_coef = lax.optimization_barrier(jnp.sum(cand_masks * (slab_grad / slab_lengths.astype(jnp.float32))[:, None], axis=0))
        sigma = jax.nn.sigmoid(outputs)
        out_grad = (token_coef[:, None, None] * readout_heads[None] * sigma * (1.0 + outputs * (1.0 - sigma))).astype(jnp.bfloat16)
        gv_scores = product_of('the,she->hts', out_grad, slab_v)
        grad_weights = jnp.where(same_cand[None], gv_scores, 0.0).astype(jnp.bfloat16)
        masked_grads = cand_masks[:, :, None, None] * out_grad[None].astype(jnp.float32)
        grad_q = scaling * (product_of('hts,shd->thd', grad_weights, slab_k) + product_of('jthe,jhde->thd', masked_grads, slab_states))
        grad_k = scaling * product_of('hts,thd->shd', grad_weights, slab_q)
        grad_v = scaling * product_of('hts,the->she', attn_weights, out_grad)
        state_grads = (scaling * product_of('jthd,the->jhde', masked_queries, out_grad)).astype(jnp.bfloat16)
        return (grad_q.astype(jnp.bfloat16), grad_k.astype(jnp.bfloat16), grad_v.astype(jnp.bfloat16), state_grads)
    cand_dq, cand_dk, cand_dv, state_grads = lax.map(cand_backward, (cand_queries, cand_keys, cand_values, cand_lengths, cand_states, raw_grad.reshape(N_SEQ, NC_DEV)))
    end_grads = jnp.zeros((PROMPTS, HEADS, E, E), jnp.float32).at[cand_prompt].add(state_grads.reshape(-1, HEADS, E, E).astype(jnp.float32))
    slot_grads = end_grads[jnp.minimum(slot_pid, PROMPTS - 1)] * valid_float[:, :, None, None, None]

    def head_terms(inputs):
        mask_one, slab_q, slab_g = inputs
        return scaling * product_of('thd,the->hde', mask_one[:, None, None] * slab_q.astype(jnp.float32), slab_g)
    head_states = lax.map(head_terms, (first_masks, queries, grads_in)) + end_flags[:, None, None, None] * slot_grads[:, 0]

    def reverse_chain(running, inputs):
        head_state, end_flag = inputs
        return (head_state + (1.0 - end_flag) * running, running)
    unused_right, from_right = lax.scan(reverse_chain, zero_state, (head_states, end_flags), reverse=True)
    right_states = jnp.concatenate([slot_grads, (cont_rights[:, None, None, None] * from_right)[:, None]], axis=1).astype(jnp.bfloat16)
    incoming_bf = incoming_first.astype(jnp.bfloat16)

    def prompt_backward(inputs):
        segment, masks_one, mask_first, slab_q, slab_k, slab_v, slab_g, incoming_one, right_one = inputs
        tok_pos = jnp.arange(P_DEV, dtype=jnp.int32)
        same_prompt = jnp.logical_and(segment[:, None] == segment[None, :], tok_pos[None, :] <= tok_pos[:, None])
        attn_prompt = jnp.where(same_prompt[None], product_of('thd,shd->hts', slab_q, slab_k), 0.0).astype(jnp.bfloat16)
        grad_prompt = jnp.where(same_prompt[None], product_of('the,she->hts', slab_g, slab_v), 0.0).astype(jnp.bfloat16)
        grad_q = scaling * (product_of('hts,shd->thd', grad_prompt, slab_k) + mask_first[:, None, None] * product_of('the,hde->thd', slab_g, incoming_one))
        grad_k = scaling * product_of('hts,thd->shd', grad_prompt, slab_q) + product_of('mshe,mhde->shd', masks_one[:, :, None, None] * slab_v[None].astype(jnp.float32), right_one)
        grad_v = scaling * product_of('hts,the->she', attn_prompt, slab_g) + product_of('mshd,mhde->she', masks_one[:, :, None, None] * slab_k[None].astype(jnp.float32), right_one)
        return (grad_q.astype(jnp.bfloat16), grad_k.astype(jnp.bfloat16), grad_v.astype(jnp.bfloat16))
    prompt_dq, prompt_dk, prompt_dv = lax.map(prompt_backward, (segments, row_masks, first_masks, queries, keys_in, values_in, grads_in, incoming_bf, right_states))
    return (prompt_dq.reshape(TOTAL, HEADS * E), prompt_dk.reshape(TOTAL, HEADS * E), prompt_dv.reshape(TOTAL, HEADS * E), cand_dq.reshape(CTOTAL, HEADS * E), cand_dk.reshape(CTOTAL, HEADS * E), cand_dv.reshape(CTOTAL, HEADS * E), list_loss)
```

```python
import functools
import math

import jax
import jax.numpy as jnp
from jax import lax
from jax.experimental import pallas as pl
from jax.experimental.pallas import tpu as pltpu
from jax.sharding import PartitionSpec as P

E = 128
LOCAL_HEADS = 4
HALF = LOCAL_HEADS // 2
RING = 4
CHUNK = 256
PIECES = 3
FAR = 1 << 30
GRAD_SCALE = 1048576.0
MESH = pl.DeviceIdType.MESH
BF = jnp.bfloat16
F32 = jnp.float32

VMEM_SPEC = pl.BlockSpec(memory_space=pltpu.VMEM)
SMEM_SPEC = pl.BlockSpec(memory_space=pltpu.SMEM)


def dot_nn(a, b):
    return lax.dot_general(a, b, (((1,), (0,)), ((), ())), preferred_element_type=F32)


def dot_nt(a, b):
    return lax.dot_general(a, b, (((1,), (1,)), ((), ())), preferred_element_type=F32)


def dot_tn(a, b):
    return lax.dot_general(a, b, (((0,), (0,)), ((), ())), preferred_element_type=F32)


def local_ends(meta_ref, ends_ref, slab, width, count):
    first = meta_ref[slab]
    last = ends_ref.shape[0] - 1
    end0 = ends_ref[jnp.minimum(first, last)] - slab * width
    end1 = jnp.where(
        first + 1 <= last, ends_ref[jnp.minimum(first + 1, last)] - slab * width, FAR
    )
    return end0, end1


class Place:
    def __init__(self):
        self.seq = lax.axis_index("seq")
        self.head = lax.axis_index("head")
        self.core = self.seq % 2
        x = (self.seq // 2) % RING
        z = self.seq // (2 * RING)
        self.pos_a = z * (1 - self.core) + x * self.core
        self.pos_b = x * (1 - self.core) + z * self.core
        self.step_a = 8 - 6 * self.core
        self.step_b = 2 + 6 * self.core

    def chip_at(self, move_a, move_b):
        return ((self.pos_a + move_a) % RING) * self.step_a + (
            (self.pos_b + move_b) % RING
        ) * self.step_b

    def neighbour(self, move_a, move_b):
        return (self.chip_at(move_a, move_b) + self.core, self.head)

    def partner(self):
        return (self.seq + 1 - 2 * self.core, self.head)

    def friends(self):
        return (
            self.neighbour(1, 0),
            self.neighbour(RING - 1, 0),
            self.neighbour(0, 1),
            self.neighbour(0, RING - 1),
            self.partner(),
        )


ROUTE_COPIES = 14


def route_scratch(slots, rows_out):
    return [
        pltpu.VMEM((RING, 2, slots, HALF, E, E), BF),
        pltpu.VMEM((RING, 2, rows_out, HALF, E, E), BF),
        pltpu.VMEM((4, rows_out, HALF, E, E), F32),
        pltpu.VMEM((2, rows_out, HALF, E, E), BF),
        pltpu.VMEM((2, 2, rows_out, HALF, E, E), BF),
        pltpu.VMEM((2, rows_out, HALF, E, E), BF),
        pltpu.VMEM((rows_out, HALF, E, E), BF),
        pltpu.SemaphoreType.DMA((ROUTE_COPIES,)),
        pltpu.SemaphoreType.DMA((ROUTE_COPIES,)),
        pltpu.SemaphoreType.DMA((1,)),
    ]


def route(place, rows_ref, rows_in, rows_out, slots, pick, scratch, between, sum_slot, zero_slot):
    gathered, parts, exact, passed, arrived, final, swapped, send, recv, local = scratch
    core = place.core
    left_a, right_a = place.neighbour(RING - 1, 0), place.neighbour(1, 0)
    left_b, right_b = place.neighbour(0, RING - 1), place.neighbour(0, 1)
    partner = place.partner()

    def remote(at, src, dst, device):
        return pltpu.make_async_remote_copy(
            src_ref=src,
            dst_ref=dst,
            send_sem=send.at[at],
            recv_sem=recv.at[at],
            device_id=device,
            device_id_type=MESH,
        )

    slot_rows = pl.ds(0, rows_in)
    mine = pltpu.make_async_copy(
        rows_ref.at[:, pl.ds(HALF * core, HALF)], gathered.at[0, core, slot_rows], local.at[0]
    )
    swap = remote(
        0,
        rows_ref.at[:, pl.ds(HALF * (1 - core), HALF)],
        gathered.at[0, core, slot_rows],
        partner,
    )
    mine.start()
    swap.start()
    for k in range(RING):
        for cc in range(2):
            gathered[k, cc, zero_slot] = jnp.zeros((HALF, E, E), BF)
    mine.wait()
    swap.wait()

    def block(k, cc):
        return gathered.at[k, cc, slot_rows]

    to_left = [remote(1 + cc, block(0, cc), block(1, cc), left_a) for cc in range(2)]
    to_right = [remote(3 + cc, block(0, cc), block(3, cc), right_a) for cc in range(2)]
    to_left[0].start()
    to_right[1].start()
    to_left[1].start()
    to_right[0].start()
    on_left = remote(5, block(1, 0), block(2, 0), left_a)
    on_right = remote(6, block(3, 1), block(2, 1), right_a)
    between(0)
    to_left[0].wait_recv()
    on_left.start()
    to_right[1].wait_recv()
    on_right.start()
    between(1)
    to_left[1].wait_recv()
    to_right[0].wait_recv()
    on_left.wait_recv()
    on_right.wait_recv()
    for copy in to_left + to_right + [on_left, on_right]:
        copy.wait_send()

    if sum_slot is not None:
        for k in range(RING):
            for cc in range(2):
                gathered[k, cc, sum_slot] = (
                    gathered[k, cc, 0].astype(F32) + gathered[k, cc, 1].astype(F32)
                ).astype(BF)

    def combine(m, cd, keep=None):
        dest = place.chip_at(0, m) + cd
        for r in range(rows_out):
            total = None
            for k in range(RING):
                for cc in range(2):
                    src = place.chip_at(k, 0) + cc
                    term = gathered[k, cc, pick(src, dest, r)].astype(F32)
                    total = term if total is None else total + term
            if keep is None:
                parts[m, cd, r] = total.astype(BF)
            else:
                exact[keep, r] = total

    far_left = remote(7, parts.at[2, 0], passed.at[0], left_b)
    far_right = remote(8, parts.at[2, 1], passed.at[1], right_b)
    left_own = remote(9, parts.at[3, 1], arrived.at[0, 1], left_b)
    right_own = remote(10, parts.at[1, 0], arrived.at[1, 0], right_b)
    left_sum = remote(11, parts.at[3, 0], arrived.at[0, 0], left_b)
    right_sum = remote(12, parts.at[1, 1], arrived.at[1, 1], right_b)
    combine(2, 0)
    far_left.start()
    combine(2, 1)
    far_right.start()
    combine(3, 1)
    left_own.start()
    combine(1, 0)
    right_own.start()
    combine(3, 0, keep=2)
    combine(1, 1, keep=3)
    far_left.wait_recv()
    parts[3, 0] = (exact[2] + passed[0].astype(F32)).astype(BF)
    left_sum.start()
    far_right.wait_recv()
    parts[1, 1] = (exact[3] + passed[1].astype(F32)).astype(BF)
    right_sum.start()
    combine(0, 0, keep=0)
    combine(0, 1, keep=1)
    between(2)
    for copy in (left_own, right_own, left_sum, right_sum):
        copy.wait_recv()
    final[...] = (
        exact[:2] + arrived[0].astype(F32) + arrived[1].astype(F32)
    ).astype(BF)
    back = remote(13, final.at[1 - core], swapped, partner)
    back.start()
    for copy in (far_left, far_right, left_own, right_own, left_sum, right_sum):
        copy.wait_send()
    back.wait()


def greet(devices):
    barrier = pltpu.get_barrier_semaphore()
    for device in devices:
        pl.semaphore_signal(barrier, inc=1, device_id=device, device_id_type=MESH)


def pieces_kernel(meta_ref, ends_ref, q_ref, k_ref, v_ref, g_ref, out_ref):
    width = q_ref.shape[0]
    slab = lax.axis_index("seq")
    end0, end1 = local_ends(meta_ref, ends_ref, slab, width, PIECES)
    spot = lax.broadcasted_iota(jnp.int32, (width, 1), 0)
    v = v_ref[...]
    zero = jnp.zeros_like(v)
    split = jnp.concatenate(
        [
            jnp.where(spot < end0, v, zero),
            jnp.where(jnp.logical_and(spot >= end0, spot < end1), v, zero),
            jnp.where(spot >= end1, v, zero),
        ],
        axis=1,
    )
    sums = dot_tn(k_ref[...], split)
    for j in range(PIECES):
        out_ref[j, 0] = sums[:, j * E : (j + 1) * E].astype(BF)
    scaling = 1.0 / math.sqrt(E * width)
    out_ref[PIECES, 0] = (
        scaling * dot_tn(q_ref[...], jnp.where(spot < end0, g_ref[...], zero))
    ).astype(BF)


def forward_kernel(meta_ref, cand_ref, rows_ref, out_ref, *scratch):
    place = Place()
    slabs = meta_ref.shape[0] // 2
    friends = place.friends()
    greet(friends)
    pl.semaphore_wait(pltpu.get_barrier_semaphore(), len(friends))

    def pick(src, dest, r):
        first = meta_ref[src]
        if r < 2:
            wanted = cand_ref[2 * dest + r]
            ok = jnp.bool_(True)
        elif r == 2:
            wanted = meta_ref[dest]
            ok = src < dest
        else:
            wanted = meta_ref[slabs + dest]
            same = jnp.logical_and(first == wanted, src > dest)
            return jnp.where(same, 3, 4)
        j = wanted - first
        found = jnp.logical_and(jnp.logical_and(j >= 0, j < PIECES), ok)
        return jnp.where(found, j, 4)

    route(place, rows_ref, 4, 4, 5, pick, scratch, lambda at: None, None, 4)
    final, swapped = scratch[5], scratch[6]
    out_ref[:, pl.ds(HALF * place.core, HALF)] = final[place.core]
    out_ref[:, pl.ds(HALF * (1 - place.core), HALF)] = swapped[...]


def cand_kernel(
    meta_ref,
    cand_ref,
    lens_ref,
    states_ref,
    q_ref,
    k_ref,
    v_ref,
    readout_ref,
    table_ref,
    dq_ref,
    dk_ref,
    dv_ref,
    right_ref,
    loss_ref,
    attn_ref,
    outs_ref,
    dout_ref,
    grads_ref,
    mine_ref,
    heads_ref,
    total_ref,
    scores_ref,
    y_send,
    y_recv,
    s_send,
    s_recv,
    *scratch,
):
    place = Place()
    slabs = meta_ref.shape[0] // 2
    planes = lax.axis_size("head")
    width = q_ref.shape[0]
    scaling = 1.0 / math.sqrt(E * 2 * width)
    barrier = pltpu.get_barrier_semaphore()

    def other_slab(at):
        return (place.seq + at) % slabs, place.head

    def hello(at, carry):
        pl.semaphore_signal(barrier, inc=1, device_id=other_slab(at), device_id_type=MESH)
        return carry

    lax.fori_loop(1, slabs, hello, 0)
    planes_other = [(place.seq, (place.head + at) % planes) for at in range(1, planes)]
    greet(planes_other)

    len0 = lens_ref[0, 0]
    len1 = lens_ref[0, 1]
    row = lax.broadcasted_iota(jnp.int32, (width, 1), 0)
    in_second = row >= len0

    def mask_of(rows, columns):
        i = lax.broadcasted_iota(jnp.int32, (width, width), 0)
        j = lax.broadcasted_iota(jnp.int32, (width, width), 1)
        apart = jnp.logical_and(i >= len0, j < len0)
        return jnp.logical_and(j <= i, jnp.logical_not(apart))

    sum_all = jnp.zeros((1, E), F32)
    sum_second = jnp.zeros((1, E), F32)
    for h in range(LOCAL_HEADS):
        cols = slice(h * E, (h + 1) * E)
        q, k, v = q_ref[:, cols], k_ref[:, cols], v_ref[:, cols]
        attn = jnp.where(mask_of(width, width), dot_nt(q, k), 0.0).astype(BF)
        attn_ref[h] = attn
        far = jnp.where(in_second, dot_nn(q, states_ref[1, h]), dot_nn(q, states_ref[0, h]))
        out = scaling * (dot_nn(attn, v) + far)
        outs_ref[h] = out
        part = out / (1.0 + jnp.exp(-out)) * readout_ref[:, cols]
        sum_all = sum_all + jnp.sum(part, axis=0, keepdims=True)
        sum_second = sum_second + jnp.sum(
            jnp.where(in_second, part, 0.0), axis=0, keepdims=True
        )
    second = jnp.sum(sum_second, axis=1, keepdims=True)
    first = jnp.sum(sum_all - sum_second, axis=1, keepdims=True)
    lane = lax.broadcasted_iota(jnp.int32, (1, E), 1)
    mine_ref[...] = jnp.where(
        lane == 0,
        first / len0.astype(F32),
        jnp.where(lane == 1, second / len1.astype(F32), 0.0),
    )
    pl.semaphore_wait(barrier, slabs - 1 + planes - 1)

    to_planes = [
        pltpu.make_async_remote_copy(
            src_ref=mine_ref,
            dst_ref=heads_ref.at[place.head],
            send_sem=y_send.at[at],
            recv_sem=y_recv.at[at],
            device_id=device,
            device_id_type=MESH,
        )
        for at, device in enumerate(planes_other)
    ]
    for copy in to_planes:
        copy.start()
    heads_ref[place.head] = mine_ref[...]
    for copy in to_planes:
        copy.wait()
    total = heads_ref[0]
    for at in range(1, planes):
        total = total + heads_ref[at]
    total_ref[...] = total

    def score_copy(at):
        return pltpu.make_async_remote_copy(
            src_ref=total_ref,
            dst_ref=scores_ref.at[place.seq],
            send_sem=s_send.at[at],
            recv_sem=s_recv.at[at],
            device_id=other_slab(at),
            device_id_type=MESH,
        )

    def tell(at, carry):
        score_copy(at).start()
        return carry

    def told(at, carry):
        score_copy(at).wait()
        return carry

    lax.fori_loop(1, slabs, tell, 0)
    scores_ref[place.seq] = total
    lax.fori_loop(1, slabs, told, 0)

    raw = scores_ref[...].reshape(slabs, E)
    prompts = lax.broadcasted_iota(jnp.int32, (slabs, E), 1)
    tanh_raw = jnp.tanh(raw)
    squashed = 3.0 * tanh_raw
    exp_scores = jnp.exp(squashed)
    table = table_ref[...]
    hot = [(table[:, j : j + 1] == prompts).astype(F32) for j in range(2)]
    weight = [jnp.exp(-table[:, 2 + j : 3 + j].astype(F32)) for j in range(2)]
    group_exp = jnp.sum(
        hot[0] * exp_scores[:, 0:1] + hot[1] * exp_scores[:, 1:2], axis=0, keepdims=True
    )
    group_weight = jnp.sum(hot[0] * weight[0] + hot[1] * weight[1], axis=0, keepdims=True)
    own_row = lax.broadcasted_iota(jnp.int32, (slabs, 1), 0) == place.seq
    loss = jnp.zeros((1, 1), F32)
    coefs = []
    for j in range(2):
        denom = jnp.sum(hot[j] * group_exp, axis=1, keepdims=True)
        target = weight[j] / jnp.sum(hot[j] * group_weight, axis=1, keepdims=True)
        score = squashed[:, j : j + 1]
        loss = loss + jnp.sum(target * (score - jnp.log(denom)), axis=0, keepdims=True)
        tanh_j = tanh_raw[:, j : j + 1]
        grad = (
            GRAD_SCALE
            / slabs
            * (exp_scores[:, j : j + 1] / denom - target)
            * 3.0
            * (1.0 - tanh_j * tanh_j)
        )
        coefs.append(jnp.sum(jnp.where(own_row, grad, 0.0), axis=0, keepdims=True))
    loss_ref[...] = -loss / slabs
    coef = jnp.where(in_second, coefs[1] / len1.astype(F32), coefs[0] / len0.astype(F32))

    for h in range(LOCAL_HEADS):
        cols = slice(h * E, (h + 1) * E)
        out = outs_ref[h]
        sigma = 1.0 / (1.0 + jnp.exp(-out))
        dout = (coef * readout_ref[:, cols] * sigma * (1.0 + out * (1.0 - sigma))).astype(BF)
        dout_ref[h] = dout
        zero = jnp.zeros_like(dout)
        split = jnp.concatenate(
            [jnp.where(in_second, zero, dout), jnp.where(in_second, dout, zero)], axis=1
        )
        sums = scaling * dot_tn(q_ref[:, cols], split)
        grads_ref[0, h] = sums[:, :E].astype(BF)
        grads_ref[1, h] = sums[:, E:].astype(BF)

    def backward(h):
        cols = slice(h * E, (h + 1) * E)
        q, k, v = q_ref[:, cols], k_ref[:, cols], v_ref[:, cols]
        dout = dout_ref[h]
        weights = jnp.where(mask_of(width, width), dot_nt(dout, v), 0.0).astype(BF)
        far = jnp.where(in_second, dot_nt(dout, states_ref[1, h]), dot_nt(dout, states_ref[0, h]))
        dq_ref[:, cols] = (scaling * (dot_nn(weights, k) + far)).astype(BF)
        dk_ref[:, cols] = (scaling * dot_tn(weights, q)).astype(BF)
        dv_ref[:, cols] = (scaling * dot_tn(attn_ref[h], dout)).astype(BF)

    def between(at):
        if at < 2:
            backward(at)
        else:
            backward(2)
            backward(3)

    def pick(src, dest, r):
        wanted = meta_ref[dest] + r
        both0 = cand_ref[2 * src] == wanted
        both1 = cand_ref[2 * src + 1] == wanted
        return jnp.where(both0, jnp.where(both1, 2, 0), jnp.where(both1, 1, 3))

    route(place, grads_ref, 2, 3, 4, pick, scratch, between, 2, 3)
    final, swapped = scratch[5], scratch[6]
    last = meta_ref[slabs + place.seq] - meta_ref[place.seq]
    for j in range(PIECES):
        use = jnp.where(last == j, 1.0, 0.0).astype(F32)
        for side, rows in ((place.core, final[place.core, j]), (1 - place.core, swapped[j])):
            heads = pl.ds(HALF * side, HALF)
            right_ref[j, heads] = (
                rows.astype(F32) + use * states_ref[3, heads].astype(F32)
            ).astype(BF)


def prompt_kernel(
    meta_ref,
    ends_ref,
    q_ref,
    k_ref,
    v_ref,
    g_ref,
    states_ref,
    right_ref,
    dq_ref,
    dk_ref,
    dv_ref,
    dk_acc,
    dv_acc,
):
    width = q_ref.shape[0]
    slab = lax.axis_index("seq")
    scaling = 1.0 / math.sqrt(E * width)
    end0, end1 = local_ends(meta_ref, ends_ref, slab, width, PIECES)

    def segment_of(spot):
        return (spot >= end0).astype(jnp.int32) + (spot >= end1).astype(jnp.int32)

    dk_acc[...] = jnp.zeros_like(dk_acc)
    dv_acc[...] = jnp.zeros_like(dv_acc)
    carry = states_ref[2, 0]
    for at in range(width // CHUNK):
        rows = slice(at * CHUNK, (at + 1) * CHUNK)
        span = (at + 1) * CHUNK
        i = lax.broadcasted_iota(jnp.int32, (CHUNK, 1), 0) + at * CHUNK
        j = lax.broadcasted_iota(jnp.int32, (1, span), 1)
        same = jnp.logical_and(segment_of(i) == segment_of(j), j <= i)
        q, g = q_ref[rows], g_ref[rows]
        attn = jnp.where(same, dot_nt(q, k_ref[:span]), 0.0).astype(BF)
        weights = jnp.where(same, dot_nt(g, v_ref[:span]), 0.0).astype(BF)
        far = jnp.where(i < end0, dot_nt(g, carry), 0.0)
        dq_ref[rows] = (scaling * (dot_nn(weights, k_ref[:span]) + far)).astype(BF)
        dk_acc[:span] += dot_tn(weights, q)
        dv_acc[:span] += dot_tn(attn, g)
    spot = lax.broadcasted_iota(jnp.int32, (width, 1), 0)
    segment = segment_of(spot)
    dk = scaling * dk_acc[...]
    dv = scaling * dv_acc[...]
    for j in range(PIECES):
        here = segment == j
        zero = jnp.zeros_like(v_ref[...])
        dk = dk + dot_nt(jnp.where(here, v_ref[...], zero), right_ref[j, 0])
        dv = dv + dot_nn(jnp.where(here, k_ref[...], zero), right_ref[j, 0])
    dk_ref[...] = dk.astype(BF)
    dv_ref[...] = dv.astype(BF)


def per_device(
    prompt_q,
    prompt_k,
    prompt_v,
    prompt_grad,
    cand_q,
    cand_k,
    cand_v,
    readout,
    prompt_ends,
    cand_lengths,
    cand_prompt,
    cand_ranks,
):
    slabs = lax.axis_size("seq")
    width = prompt_q.shape[0]
    cand_width = cand_q.shape[0]
    flat = prompt_q.shape[1]
    starts = jnp.arange(slabs, dtype=jnp.int32) * width
    marks = jnp.concatenate([starts, starts + (width - 1)])
    meta = jnp.sum((prompt_ends[None, :] <= marks[:, None]).astype(jnp.int32), axis=1)
    table = jnp.concatenate(
        [cand_prompt.reshape(slabs, 2), cand_ranks.reshape(slabs, 2)], axis=1
    )
    head_block = pl.BlockSpec((width, E), lambda h: (0, h))

    rows = pl.pallas_call(
        pieces_kernel,
        grid=(LOCAL_HEADS,),
        out_shape=jax.ShapeDtypeStruct((4, LOCAL_HEADS, E, E), BF),
        in_specs=[SMEM_SPEC, SMEM_SPEC, head_block, head_block, head_block, head_block],
        out_specs=pl.BlockSpec((4, 1, E, E), lambda h: (0, h, 0, 0)),
        name="pieces",
    )(meta, prompt_ends, prompt_q, prompt_k, prompt_v, prompt_grad)

    states = pl.pallas_call(
        forward_kernel,
        out_shape=jax.ShapeDtypeStruct((4, LOCAL_HEADS, E, E), BF),
        in_specs=[SMEM_SPEC, SMEM_SPEC, VMEM_SPEC],
        out_specs=VMEM_SPEC,
        scratch_shapes=route_scratch(5, 4),
        compiler_params=pltpu.CompilerParams(
            collective_id=0, has_side_effects=True, vmem_limit_bytes=48 << 20
        ),
        name="route_states",
    )(meta, cand_prompt, rows)

    cand_shape = jax.ShapeDtypeStruct((cand_width, flat), BF)
    cand_dq, cand_dk, cand_dv, right, loss = pl.pallas_call(
        cand_kernel,
        out_shape=(
            cand_shape,
            cand_shape,
            cand_shape,
            jax.ShapeDtypeStruct((PIECES, LOCAL_HEADS, E, E), BF),
            jax.ShapeDtypeStruct((1, 1), F32),
        ),
        in_specs=[SMEM_SPEC, SMEM_SPEC, SMEM_SPEC] + [VMEM_SPEC] * 6,
        out_specs=[VMEM_SPEC] * 5,
        scratch_shapes=[
            pltpu.VMEM((LOCAL_HEADS, cand_width, cand_width), BF),
            pltpu.VMEM((LOCAL_HEADS, cand_width, E), F32),
            pltpu.VMEM((LOCAL_HEADS, cand_width, E), BF),
            pltpu.VMEM((2, LOCAL_HEADS, E, E), BF),
            pltpu.VMEM((1, E), F32),
            pltpu.VMEM((4, 1, E), F32),
            pltpu.VMEM((1, E), F32),
            pltpu.VMEM((slabs, 1, E), F32),
            pltpu.SemaphoreType.DMA((3,)),
            pltpu.SemaphoreType.DMA((3,)),
            pltpu.SemaphoreType.DMA((slabs,)),
            pltpu.SemaphoreType.DMA((slabs,)),
        ]
        + route_scratch(4, 3),
        compiler_params=pltpu.CompilerParams(
            collective_id=1, has_side_effects=True, vmem_limit_bytes=48 << 20
        ),
        name="candidates",
    )(
        meta,
        cand_prompt,
        cand_lengths,
        states,
        cand_q,
        cand_k,
        cand_v,
        readout.reshape(1, flat),
        table,
    )

    row_block = lambda rows: pl.BlockSpec((rows, 1, E, E), lambda h: (0, h, 0, 0))
    prompt_shape = jax.ShapeDtypeStruct((width, flat), BF)
    prompt_dq, prompt_dk, prompt_dv = pl.pallas_call(
        prompt_kernel,
        grid=(LOCAL_HEADS,),
        out_shape=(prompt_shape,) * 3,
        in_specs=[
            SMEM_SPEC,
            SMEM_SPEC,
            head_block,
            head_block,
            head_block,
            head_block,
            row_block(4),
            row_block(PIECES),
        ],
        out_specs=(head_block,) * 3,
        scratch_shapes=[pltpu.VMEM((width, E), F32)] * 2,
        name="prompt_backward",
    )(meta, prompt_ends, prompt_q, prompt_k, prompt_v, prompt_grad, states, right)

    return (
        prompt_dq,
        prompt_dk,
        prompt_dv,
        cand_dq,
        cand_dk,
        cand_dv,
        loss.reshape(()),
    )


def solution(mesh):
    both = P("seq", "head")
    return jax.shard_map(
        per_device,
        mesh=mesh,
        in_specs=(
            both,
            both,
            both,
            both,
            both,
            both,
            both,
            P("head"),
            P(),
            P("seq", None),
            P(),
            P(),
        ),
        out_specs=(both, both, both, both, both, both, P()),
        check_vma=False,
    )
```

```python
import functools
import math

import jax
import jax.numpy as jnp
from jax import lax
from jax.experimental import pallas as pl
from jax.experimental.pallas import tpu as pltpu
from jax.sharding import PartitionSpec as P

E = 128
LOCAL_HEADS = 4
HALF = LOCAL_HEADS // 2
RING = 4
CHUNK = 256
PIECES = 3
CHIP_ROWS = 5
CHIP_ENDS = 4
SUM01, SUM23, NONE = 4, 5, 6
FAR = 1 << 30
GRAD_SCALE = 1048576.0
MESH = pl.DeviceIdType.MESH
BF = jnp.bfloat16
F32 = jnp.float32

VMEM_SPEC = pl.BlockSpec(memory_space=pltpu.VMEM)
SMEM_SPEC = pl.BlockSpec(memory_space=pltpu.SMEM)


def dot_nn(a, b):
    return lax.dot_general(a, b, (((1,), (0,)), ((), ())), preferred_element_type=F32)


def dot_nt(a, b):
    return lax.dot_general(a, b, (((1,), (1,)), ((), ())), preferred_element_type=F32)


def dot_tn(a, b):
    return lax.dot_general(a, b, (((0,), (0,)), ((), ())), preferred_element_type=F32)


def local_ends(meta_ref, ends_ref, slab, width, count):
    first = meta_ref[slab]
    last = ends_ref.shape[0] - 1
    end0 = ends_ref[jnp.minimum(first, last)] - slab * width
    end1 = jnp.where(
        first + 1 <= last, ends_ref[jnp.minimum(first + 1, last)] - slab * width, FAR
    )
    return end0, end1


class Place:
    def __init__(self):
        self.seq = lax.axis_index("seq")
        self.head = lax.axis_index("head")
        self.core = self.seq % 2
        x = (self.seq // 2) % RING
        z = self.seq // (2 * RING)
        self.pos_a = z * (1 - self.core) + x * self.core
        self.pos_b = x * (1 - self.core) + z * self.core
        self.step_a = 8 - 6 * self.core
        self.step_b = 2 + 6 * self.core

    def chip_at(self, move_a, move_b):
        return ((self.pos_a + move_a) % RING) * self.step_a + (
            (self.pos_b + move_b) % RING
        ) * self.step_b

    def neighbour(self, move_a, move_b):
        return (self.chip_at(move_a, move_b) + self.core, self.head)

    def partner(self):
        return (self.seq + 1 - 2 * self.core, self.head)


class Spread:
    COPIES = 6

    @staticmethod
    def scratch(rows, kind):
        return [
            pltpu.VMEM((RING, HALF, rows, E, E), kind),
            pltpu.VMEM((2, rows, E, E), F32),
            pltpu.VMEM((HALF, rows, E, E), kind),
            pltpu.VMEM((2, HALF, rows, E, E), kind),
            pltpu.SemaphoreType.DMA((Spread.COPIES,)),
            pltpu.SemaphoreType.DMA((Spread.COPIES,)),
        ]

    def __init__(self, place, rows, scratch, term):
        self.rows, self.term = rows, term
        self.parts, self.exact, self.passed, self.arrived, send, recv = scratch
        left, right = place.neighbour(0, RING - 1), place.neighbour(0, 1)
        parts, passed, arrived = self.parts, self.passed, self.arrived
        pairs = (
            (parts.at[2, 0], passed.at[0], left),
            (parts.at[2, 1], passed.at[1], right),
            (parts.at[3, 1], arrived.at[0, 1], left),
            (parts.at[1, 0], arrived.at[1, 0], right),
            (parts.at[3, 0], arrived.at[0, 0], left),
            (parts.at[1, 1], arrived.at[1, 1], right),
        )
        self.copies = [
            remote_copy(src, dst, send.at[at], recv.at[at], device)
            for at, (src, dst, device) in enumerate(pairs)
        ]

    def begin(self):
        for at, (m, i) in enumerate(((2, 0), (2, 1), (3, 1), (1, 0))):
            for r in range(self.rows):
                self.parts[m, i, r] = self.term(m, i, r).astype(self.parts.dtype)
            self.copies[at].start()

    def pass_on(self):
        for at, (m, i) in enumerate(((3, 0), (1, 1))):
            for r in range(self.rows):
                self.exact[at, r] = self.term(m, i, r).astype(F32)
        for at, (m, i) in enumerate(((3, 0), (1, 1))):
            self.copies[at].wait_recv()
            for r in range(self.rows):
                self.parts[m, i, r] = (
                    self.exact[at, r] + self.passed[i, r].astype(F32)
                ).astype(self.parts.dtype)
            self.copies[4 + at].start()

    def arrive(self):
        for copy in self.copies[2:]:
            copy.wait_recv()

    def result(self, i, r):
        return (
            self.term(0, i, r).astype(F32)
            + self.arrived[0, i, r].astype(F32)
            + self.arrived[1, i, r].astype(F32)
        )

    def finish(self):
        for copy in self.copies:
            copy.wait_send()


class Gather:
    COPIES = 6

    def __init__(self, place, block, send, recv):
        left, right = place.neighbour(RING - 1, 0), place.neighbour(1, 0)
        pairs = (
            (block(0, 0), block(1, 0), left),
            (block(0, 1), block(3, 1), right),
            (block(0, 1), block(1, 1), left),
            (block(0, 0), block(3, 0), right),
            (block(1, 0), block(2, 0), left),
            (block(3, 1), block(2, 1), right),
        )
        self.copies = [
            remote_copy(src, dst, send.at[at], recv.at[at], device)
            for at, (src, dst, device) in enumerate(pairs)
        ]

    def begin(self):
        for copy in self.copies[:4]:
            copy.start()

    def pass_on(self):
        for at in range(2):
            self.copies[at].wait_recv()
            self.copies[4 + at].start()

    def arrive(self):
        for copy in self.copies[2:]:
            copy.wait_recv()
        for copy in self.copies:
            copy.wait_send()


def remote_copy(src, dst, send, recv, device):
    return pltpu.make_async_remote_copy(
        src_ref=src,
        dst_ref=dst,
        send_sem=send,
        recv_sem=recv,
        device_id=device,
        device_id_type=MESH,
    )


def flag(condition):
    return jnp.where(condition, 1.0, 0.0).astype(F32)


def lanes(head):
    return pl.ds(pl.multiple_of(head * E, E), E)


def main_kernel(
    meta_ref,
    ends_ref,
    cand_ref,
    lens_ref,
    ranks_ref,
    readout_ref,
    pq_hbm,
    pk_hbm,
    pv_hbm,
    pg_hbm,
    cq_hbm,
    ck_hbm,
    cv_hbm,
    dq_hbm,
    dkp_hbm,
    dvp_hbm,
    cdq_hbm,
    cdk_hbm,
    cdv_hbm,
    right_ref,
    loss_ref,
    pq,
    pk,
    pv,
    pg,
    cq,
    ck,
    cv,
    masks,
    dq_acc,
    dkp,
    dvp,
    dq_out,
    cdq,
    cdk,
    cdv,
    own,
    theirs,
    mail,
    qg_own,
    qg_theirs,
    qg_mail,
    states,
    states_mail,
    states_in,
    carry_mail,
    carry_in,
    carry,
    chip_carry,
    right_sum,
    right_mail,
    right_in,
    attn_ref,
    outs_ref,
    dout_ref,
    grads_mail,
    mine_ref,
    heads_ref,
    total_ref,
    scores_ref,
    gathered,
    gathered_wide,
    gathered_qg,
    gathered_grads,
    table_ref,
    in_sem,
    out_sem,
    swap_send,
    swap_recv,
    ring_send,
    ring_recv,
    y_send,
    y_recv,
    s_send,
    s_recv,
    *spread_scratch,
):
    place = Place()
    core = place.core
    slabs = meta_ref.shape[0] // 2
    planes = lax.axis_size("head")
    width = pq.shape[0]
    cand_width = cq.shape[0]
    scaling = 1.0 / math.sqrt(E * width)
    barrier = pltpu.get_barrier_semaphore()

    def other_slab(at):
        return (place.seq + at) % slabs, place.head

    def hello(at, held):
        pl.semaphore_signal(barrier, inc=1, device_id=other_slab(at), device_id_type=MESH)
        return held

    loads = [
        pltpu.make_async_copy(src, dst, in_sem.at[at])
        for at, (src, dst) in enumerate(
            (
                (pk_hbm, pk),
                (pv_hbm, pv),
                (pg_hbm, pg),
                (pq_hbm, pq),
                (cq_hbm, cq),
                (ck_hbm, ck),
                (cv_hbm, cv),
            )
        )
    ]
    loads[0].start()
    loads[1].start()
    lax.fori_loop(1, slabs, hello, 0)
    planes_other = [(place.seq, (place.head + at) % planes) for at in range(1, planes)]
    for device in planes_other:
        pl.semaphore_signal(barrier, inc=1, device_id=device, device_id_type=MESH)

    def store(at, src, dst):
        copy = pltpu.make_async_copy(src, dst, out_sem.at[at])
        copy.start()
        return copy

    def swap(at, src, dst):
        return remote_copy(src, dst, swap_send.at[at], swap_recv.at[at], place.partner())

    end0, end1 = local_ends(meta_ref, ends_ref, place.seq, width, PIECES)
    spot = lax.broadcasted_iota(jnp.int32, (width, E), 0)
    masks[0] = flag(spot < end0).astype(BF)
    masks[1] = flag(jnp.logical_and(spot >= end0, spot < end1)).astype(BF)
    masks[2] = flag(spot >= end1).astype(BF)

    def piece_sums(head):
        v = pv[:, lanes(head)]
        split = jnp.concatenate([v * masks[j] for j in range(PIECES)], axis=1)
        return dot_tn(pk[:, lanes(head)], split)

    loads[0].wait()
    loads[1].wait()
    for load in loads[2:]:
        load.start()
    pieces_swaps = []
    for i in range(HALF):
        sums = piece_sums(HALF * (1 - core) + i)
        for j in range(PIECES):
            mail[i, j] = sums[:, j * E : (j + 1) * E]
        if i == 0:
            pl.semaphore_wait(barrier, slabs - 1 + planes - 1)
        pieces_swaps.append(swap(6 * i, mail.at[i], theirs.at[i, pl.ds(0, PIECES)]))
        pieces_swaps[-1].start()
    for i in range(HALF):
        sums = piece_sums(HALF * core + i)
        for j in range(PIECES):
            own[j, i] = sums[:, j * E : (j + 1) * E]
        own[PIECES, i] = jnp.zeros((E, E), F32)
        theirs[i, PIECES] = jnp.zeros((E, E), F32)
        for k in range(RING):
            gathered[k, i, CHIP_ENDS - 1] = jnp.zeros((E, E), BF)
            gathered_wide[k, i, 2] = jnp.zeros((E, E), F32)
            gathered_grads[k, i, NONE] = jnp.zeros((E, E), BF)

    chip = place.chip_at(0, 0)
    first0, first1 = meta_ref[chip], meta_ref[chip + 1]
    last0, last1 = meta_ref[slabs + chip], meta_ref[slabs + chip + 1]
    off = jnp.clip(first1 - first0, 0, PIECES - 1)
    off_own, off_theirs = off * core, off * (1 - core)

    def slot_in(j, count):
        return jnp.where(jnp.logical_and(j >= 0, j < count), j, count)

    def chip_row(i, j):
        at_own, at_theirs = slot_in(j - off_own, PIECES), slot_in(j - off_theirs, PIECES)
        return own[at_own, i] + theirs[i, at_theirs]

    tail0 = jnp.where(last0 == last1, slot_in(last0 - first0, PIECES), PIECES)
    tail1 = slot_in(last1 - first1, PIECES)
    tail_own = jnp.where(core == 0, tail0, tail1)
    tail_theirs = jnp.where(core == 0, tail1, tail0)
    wide_ring = Gather(
        place,
        lambda k, i: gathered_wide.at[k, i, pl.ds(0, 2)],
        ring_send.at[0],
        ring_recv.at[0],
    )
    ends_ring = Gather(
        place,
        lambda k, i: gathered.at[k, i, pl.ds(0, CHIP_ENDS - 1)],
        ring_send.at[1],
        ring_recv.at[1],
    )
    for copy in pieces_swaps:
        copy.wait()
    for i in range(HALF):
        gathered_wide[0, i, 0] = chip_row(i, 0)
        gathered_wide[0, i, 1] = own[tail_own, i] + theirs[i, tail_theirs]
    wide_ring.begin()
    for i in range(HALF):
        for j in range(1, CHIP_ENDS):
            gathered[0, i, j - 1] = chip_row(i, j).astype(BF)
    ends_ring.begin()

    def segment_of(at):
        return (at >= end0).astype(jnp.int32) + (at >= end1).astype(jnp.int32)

    def prompt_task(at, low, high):
        rows = slice(at * CHUNK, (at + 1) * CHUNK)
        span = (at + 1) * CHUNK
        i = lax.broadcasted_iota(jnp.int32, (CHUNK, 1), 0) + at * CHUNK
        j = lax.broadcasted_iota(jnp.int32, (1, span), 1)
        same = jnp.logical_and(segment_of(i) == segment_of(j), j <= i)

        def one(h, held):
            cols = lanes(h)
            q, g = pq[rows, cols], pg[rows, cols]
            attn = jnp.where(same, dot_nt(q, pk[:span, cols]), 0.0).astype(BF)
            weights = jnp.where(same, dot_nt(g, pv[:span, cols]), 0.0).astype(BF)
            dq_acc[rows, cols] = dot_nn(weights, pk[:span, cols])
            dk = scaling * dot_tn(weights, q)
            dv = scaling * dot_tn(attn, g)
            if span == width:
                dkp[:, cols] = dk
                dvp[:, cols] = dv
            else:
                dkp[:span, cols] += dk
                dvp[:span, cols] += dv
            return held

        lax.fori_loop(low, high, one, 0)

    len0 = lens_ref[0, 0]
    len1 = lens_ref[0, 1]
    in_second = lax.broadcasted_iota(jnp.int32, (cand_width, 1), 0) >= len0

    def same_cand():
        i = lax.broadcasted_iota(jnp.int32, (cand_width, 1), 0)
        j = lax.broadcasted_iota(jnp.int32, (1, cand_width), 1)
        return jnp.logical_and(j <= i, (i >= len0).astype(jnp.int32) == (j >= len0).astype(jnp.int32))

    def cand_near(low, high):
        if low == 0:
            for load in loads[4:]:
                load.wait()

        def one(h, held):
            cols = lanes(h)
            attn = jnp.where(same_cand(), dot_nt(cq[:, cols], ck[:, cols]), 0.0).astype(BF)
            attn_ref[h] = attn
            outs_ref[h] = dot_nn(attn, cv[:, cols])
            return held

        lax.fori_loop(low, high, one, 0)

    def cand_backward(low, high):
        def one(h, held):
            cols = lanes(h)
            dout = dout_ref[h]
            weights = jnp.where(same_cand(), dot_nt(dout, cv[:, cols]), 0.0).astype(BF)
            far = jnp.where(in_second, dot_nt(dout, states[1, h]), dot_nt(dout, states[0, h]))
            cdq[:, cols] = (scaling * (dot_nn(weights, ck[:, cols]) + far)).astype(BF)
            cdk[:, cols] = (scaling * dot_tn(weights, cq[:, cols])).astype(BF)
            cdv[:, cols] = (scaling * dot_tn(attn_ref[h], dout)).astype(BF)
            return held

        lax.fori_loop(low, high, one, 0)

    def dq_finish():
        def one(h, held):
            cols = lanes(h)
            far = dot_nt(pg[:, cols], carry[h])
            inside = lax.broadcasted_iota(jnp.int32, (width, 1), 0) < end0
            dq_out[:, cols] = (scaling * (dq_acc[:, cols] + jnp.where(inside, far, 0.0))).astype(BF)
            return held

        lax.fori_loop(0, LOCAL_HEADS, one, 0)

    loads[2].wait()
    loads[3].wait()

    def qg_sum(head):
        return scaling * dot_tn(pq[:, lanes(head)], pg[:, lanes(head)] * masks[0])

    for i in range(HALF):
        qg_mail[i] = qg_sum(HALF * (1 - core) + i)
    qg_swap = swap(1, qg_mail, qg_theirs)
    qg_swap.start()
    for i in range(HALF):
        qg_own[i] = qg_sum(HALF * core + i)
    wide_ring.pass_on()
    ends_ring.pass_on()
    prompt_task(3, 0, 3)
    whole = flag(off == 0)

    def carry_term(m, i):
        dest = place.chip_at(0, m)
        total = None
        for k in range(RING):
            src = place.chip_at(k, 0)
            same = jnp.logical_and(meta_ref[slabs + src + 1] == meta_ref[dest], src < dest)
            term = gathered_wide[k, i, jnp.where(same, 1, 2)]
            total = term if total is None else total + term
        return total

    def memory_term(m, i, r):
        if r == 0:
            return carry_term(m, i)
        dest = place.chip_at(0, m)
        total = None
        for k in range(RING):
            src = place.chip_at(k, 0)
            same = jnp.logical_and(meta_ref[src] == meta_ref[slabs + dest + 1], src > dest)
            term = flag(same) * gathered_qg[k, i]
            total = term if total is None else total + term
        return total

    def state_term(m, i, r):
        wanted = cand_ref[2 * place.chip_at(0, m) + r]
        source = jnp.clip((ends_ref[wanted] - 1) // (2 * width), 0, slabs // 2 - 1)
        src_z, src_x = source // RING, source % RING
        src_a = jnp.where(core == 0, src_z, src_x)
        src_b = jnp.where(core == 0, src_x, src_z)
        k_end = (src_a - place.pos_a + RING) % RING
        row = wanted - meta_ref[2 * source]
        inner = jnp.logical_and(src_b == place.pos_b, row > 0)
        total = gathered[k_end, i, jnp.where(inner, jnp.minimum(row - 1, CHIP_ENDS - 2), CHIP_ENDS - 1)].astype(F32)
        for k in range(RING):
            src = place.chip_at(k, 0)
            opens = jnp.logical_and(src < 2 * source, meta_ref[slabs + src + 1] == wanted)
            ends = jnp.logical_and(src == 2 * source, row == 0)
            total = total + gathered_wide[k, i, jnp.where(opens, 1, jnp.where(ends, 0, 2))]
        return total

    def grad_term(m, i, r):
        wanted = meta_ref[place.chip_at(0, m)] + r
        total = None
        for k in range(RING):
            src = 2 * place.chip_at(k, 0)
            is0, is1, is2, is3 = [cand_ref[src + c] == wanted for c in range(4)]
            slot0 = jnp.where(is0, jnp.where(is1, SUM01, 0), jnp.where(is1, 1, NONE))
            slot1 = jnp.where(is2, jnp.where(is3, SUM23, 2), jnp.where(is3, 3, NONE))
            term = gathered_grads[k, i, slot0].astype(F32) + gathered_grads[k, i, slot1].astype(F32)
            total = term if total is None else total + term
        return total

    to_states = Spread(place, 4, spread_scratch[:6], state_term)
    to_memory = Spread(place, 2, spread_scratch[6:12], memory_term)
    to_grads = Spread(place, CHIP_ROWS, spread_scratch[12:], grad_term)

    qg_swap.wait()
    own_scale = jnp.where(core == 0, 1.0, whole)
    their_scale = jnp.where(core == 0, whole, 1.0)
    for i in range(HALF):
        gathered_qg[0, i] = own_scale * qg_own[i] + their_scale * qg_theirs[i]
    wide_ring.arrive()
    ends_ring.arrive()
    to_states.begin()
    cand_near(0, 2)
    to_states.pass_on()
    qg_ring = Gather(place, lambda k, i: gathered_qg.at[k, i], ring_send.at[2], ring_recv.at[2])
    qg_ring.begin()
    cand_near(2, 4)
    qg_ring.pass_on()
    prompt_task(3, 3, 4)
    to_states.arrive()
    for i in range(HALF):
        for r in range(2):
            states_mail[i, r] = to_states.result(i, 2 * (1 - core) + r).astype(BF)
    states_swap = swap(2, states_mail, states_in)
    states_swap.start()
    for i in range(HALF):
        for r in range(2):
            states[r, HALF * core + i] = to_states.result(i, 2 * core + r).astype(BF)
    qg_ring.arrive()
    to_memory.begin()
    states_swap.wait()
    for i in range(HALF):
        for r in range(2):
            states[r, HALF * (1 - core) + i] = states_in[i, r]

    sum_all = jnp.zeros((1, E), F32)
    sum_second = jnp.zeros((1, E), F32)
    for h in range(LOCAL_HEADS):
        cols = slice(h * E, (h + 1) * E)
        far = jnp.where(
            in_second, dot_nn(cq[:, cols], states[1, h]), dot_nn(cq[:, cols], states[0, h])
        )
        out = scaling * (outs_ref[h] + far)
        outs_ref[h] = out
        part = out / (1.0 + jnp.exp(-out)) * readout_ref[:, cols]
        sum_all = sum_all + jnp.sum(part, axis=0, keepdims=True)
        sum_second = sum_second + jnp.sum(jnp.where(in_second, part, 0.0), axis=0, keepdims=True)
    second = jnp.sum(sum_second, axis=1, keepdims=True)
    first = jnp.sum(sum_all - sum_second, axis=1, keepdims=True)
    lane = lax.broadcasted_iota(jnp.int32, (1, E), 1)
    mine_ref[...] = jnp.where(
        lane == 0,
        first / len0.astype(F32),
        jnp.where(lane == 1, second / len1.astype(F32), 0.0),
    )
    to_planes = [
        remote_copy(mine_ref, heads_ref.at[place.head], y_send.at[at], y_recv.at[at], device)
        for at, device in enumerate(planes_other)
    ]
    for copy in to_planes:
        copy.start()
    heads_ref[place.head] = mine_ref[...]
    to_memory.pass_on()
    for copy in to_planes:
        copy.wait()
    total = heads_ref[0]
    for at in range(1, planes):
        total = total + heads_ref[at]
    total_ref[...] = total

    def score_copy(at):
        return remote_copy(
            total_ref, scores_ref.at[place.seq], s_send.at[at], s_recv.at[at], other_slab(at)
        )

    def tell(at, held):
        score_copy(at).start()
        return held

    def told(at, held):
        score_copy(at).wait()
        return held

    def build_table():
        rows = lax.broadcasted_iota(jnp.int32, (slabs, E), 0)

        def one(at, held):
            here = rows == at
            values = (
                cand_ref[2 * at],
                cand_ref[2 * at + 1],
                ranks_ref[2 * at],
                ranks_ref[2 * at + 1],
            )
            return tuple(jnp.where(here, value, old) for value, old in zip(values, held))

        blank = jnp.zeros((slabs, E), jnp.int32)
        for at, plane in enumerate(lax.fori_loop(0, slabs, one, (blank,) * 4)):
            table_ref[at] = plane

    lax.fori_loop(1, slabs, tell, 0)
    scores_ref[place.seq] = total
    build_table()
    prompt_task(2, 0, 3)
    lax.fori_loop(1, slabs, told, 0)

    raw = scores_ref[...].reshape(slabs, E)
    prompts = lax.broadcasted_iota(jnp.int32, (slabs, E), 1)
    tanh_raw = jnp.tanh(raw)
    squashed = 3.0 * tanh_raw
    exp_scores = jnp.exp(squashed)
    hot = [(table_ref[j] == prompts).astype(F32) for j in range(2)]
    weight = [jnp.exp(-table_ref[2 + j].astype(F32)) for j in range(2)]
    group_exp = jnp.sum(
        hot[0] * exp_scores[:, 0:1] + hot[1] * exp_scores[:, 1:2], axis=0, keepdims=True
    )
    group_weight = jnp.sum(hot[0] * weight[0] + hot[1] * weight[1], axis=0, keepdims=True)
    own_row = lax.broadcasted_iota(jnp.int32, (slabs, 1), 0) == place.seq
    loss = jnp.zeros((1, 1), F32)
    coefs = []
    for j in range(2):
        denom = jnp.sum(hot[j] * group_exp, axis=1, keepdims=True)
        target = weight[j][:, 0:1] / jnp.sum(hot[j] * group_weight, axis=1, keepdims=True)
        score = squashed[:, j : j + 1]
        loss = loss + jnp.sum(target * (score - jnp.log(denom)), axis=0, keepdims=True)
        tanh_j = tanh_raw[:, j : j + 1]
        grad = (
            GRAD_SCALE
            / slabs
            * (exp_scores[:, j : j + 1] / denom - target)
            * 3.0
            * (1.0 - tanh_j * tanh_j)
        )
        coefs.append(jnp.sum(jnp.where(own_row, grad, 0.0), axis=0, keepdims=True))
    loss_ref[...] = -loss / slabs
    coef = jnp.where(in_second, coefs[1] / len1.astype(F32), coefs[0] / len0.astype(F32))

    def grad_sums(h):
        out = outs_ref[h]
        sigma = 1.0 / (1.0 + jnp.exp(-out))
        slope = coef * readout_ref[:, lanes(h)] * sigma * (1.0 + out * (1.0 - sigma))
        dout_ref[h] = slope.astype(BF)
        split = jnp.concatenate(
            [
                jnp.where(in_second, 0.0, slope).astype(BF),
                jnp.where(in_second, slope, 0.0).astype(BF),
            ],
            axis=1,
        )
        return scaling * dot_tn(cq[:, lanes(h)], split)

    for i in range(HALF):
        sums = grad_sums(HALF * (1 - core) + i)
        for r in range(2):
            grads_mail[i, r] = sums[:, r * E : (r + 1) * E].astype(BF)
    own_slots = pl.ds(2 * core, 2)
    grads_swap = swap(3, grads_mail, gathered_grads.at[0, :, own_slots])
    grads_swap.start()
    for i in range(HALF):
        sums = grad_sums(HALF * core + i)
        for r in range(2):
            gathered_grads[0, i, 2 * core + r] = sums[:, r * E : (r + 1) * E].astype(BF)
    grads_swap.wait()
    grads_ring = Gather(
        place,
        lambda k, i: gathered_grads.at[k, i, pl.ds(0, 4)],
        ring_send.at[3],
        ring_recv.at[3],
    )
    grads_ring.begin()

    to_memory.arrive()
    seam = slot_in(off, PIECES)

    def carry_row(i, at_core):
        before = jnp.where(core == 0, own[seam, i], theirs[i, seam])
        is_second = flag(at_core == 1)
        keep = jnp.where(at_core == 0, 1.0, whole)
        return (keep * chip_carry[i] + is_second * before).astype(BF)

    for i in range(HALF):
        chip_carry[i] = to_memory.result(i, 0)
        carry_mail[i] = carry_row(i, 1 - core)
    carry_swap = swap(4, carry_mail, carry_in)
    carry_swap.start()
    for i in range(HALF):
        carry[HALF * core + i] = carry_row(i, core)
    cand_backward(0, 2)
    grads_ring.pass_on()
    cand_backward(2, 4)
    outputs = [store(0, cdq, cdq_hbm), store(1, cdk, cdk_hbm), store(2, cdv, cdv_hbm)]
    carry_swap.wait()
    for i in range(HALF):
        carry[HALF * (1 - core) + i] = carry_in[i]
    grads_ring.arrive()
    for k in range(RING):
        for i in range(HALF):
            for target, source in ((SUM01, 0), (SUM23, 2)):
                gathered_grads[k, i, target] = (
                    gathered_grads[k, i, source].astype(F32)
                    + gathered_grads[k, i, source + 1].astype(F32)
                ).astype(BF)
    to_grads.begin()
    to_grads.pass_on()
    prompt_task(2, 3, 4)
    prompt_task(1, 0, 4)
    prompt_task(0, 0, 4)
    outputs += [store(3, dkp, dkp_hbm), store(4, dvp, dvp_hbm)]
    dq_finish()
    outputs.append(store(5, dq_out, dq_hbm))
    to_grads.arrive()
    for i in range(HALF):
        for r in range(CHIP_ROWS):
            right_sum[r, i] = to_grads.result(i, r)

    def later_row(i, at_core):
        chip_later = to_memory.result(i, 1)
        second_qg = jnp.where(core == 0, qg_theirs[i], qg_own[i])
        inner = flag(first1 == last0) * second_qg + flag(last1 == last0) * chip_later
        return jnp.where(at_core == 0, inner, chip_later)

    def right_row(i, j, at_core, later):
        into = jnp.where(at_core == 0, last0 - first0, last1 - first1)
        return (right_sum[j + off * at_core, i] + flag(into == j) * later).astype(BF)

    for i in range(HALF):
        later = later_row(i, 1 - core)
        for j in range(PIECES):
            right_mail[j, i] = right_row(i, j, 1 - core, later)
    right_swap = swap(5, right_mail, right_in)
    right_swap.start()
    for i in range(HALF):
        later = later_row(i, core)
        for j in range(PIECES):
            right_ref[j, HALF * core + i] = right_row(i, j, core, later)
    for spread in (to_states, to_memory, to_grads):
        spread.finish()
    right_swap.wait()
    for i in range(HALF):
        for j in range(PIECES):
            right_ref[j, HALF * (1 - core) + i] = right_in[j, i]
    for copy in outputs:
        copy.wait()


def last_kernel(
    meta_ref,
    ends_ref,
    k_ref,
    v_ref,
    dkp_ref,
    dvp_ref,
    right_ref,
    dq_in,
    cdq_in,
    cdk_in,
    cdv_in,
    dq_ref,
    dk_ref,
    dv_ref,
    cdq_ref,
    cdk_ref,
    cdv_ref,
):
    width = k_ref.shape[0]
    slab = lax.axis_index("seq")
    end0, end1 = local_ends(meta_ref, ends_ref, slab, width, PIECES)
    spot = lax.broadcasted_iota(jnp.int32, (width, 1), 0)
    k, v = k_ref[...], v_ref[...]
    dk = [dot_nt(v, right_ref[j, 0]) for j in range(PIECES)]
    dv = [dot_nn(k, right_ref[j, 0]) for j in range(PIECES)]
    for out, part, far in ((dk_ref, dkp_ref, dk), (dv_ref, dvp_ref, dv)):
        chosen = jnp.where(spot < end0, far[0], jnp.where(spot < end1, far[1], far[2]))
        out[...] = (part[...] + chosen).astype(BF)
    dq_ref[...] = dq_in[...]
    cdq_ref[...] = cdq_in[...]
    cdk_ref[...] = cdk_in[...]
    cdv_ref[...] = cdv_in[...]


def per_device(
    prompt_q,
    prompt_k,
    prompt_v,
    prompt_grad,
    cand_q,
    cand_k,
    cand_v,
    readout,
    prompt_ends,
    cand_lengths,
    cand_prompt,
    cand_ranks,
):
    slabs = lax.axis_size("seq")
    width = prompt_q.shape[0]
    cand_width = cand_q.shape[0]
    flat = prompt_q.shape[1]
    starts = jnp.arange(slabs, dtype=jnp.int32) * width
    marks = jnp.concatenate([starts, starts + (width - 1)])
    meta = jnp.sum((prompt_ends[None, :] <= marks[:, None]).astype(jnp.int32), axis=1)
    any_spec = pl.BlockSpec(memory_space=pl.ANY)
    prompt_shape = jax.ShapeDtypeStruct((width, flat), BF)
    prompt_wide = jax.ShapeDtypeStruct((width, flat), F32)
    cand_shape = jax.ShapeDtypeStruct((cand_width, flat), BF)
    prompt_buf = pltpu.VMEM((width, flat), BF)
    prompt_acc = pltpu.VMEM((width, flat), F32)
    cand_buf = pltpu.VMEM((cand_width, flat), BF)
    half_rows = lambda *lead, kind=BF: pltpu.VMEM(lead + (E, E), kind)
    dma = pltpu.SemaphoreType.DMA
    dq_part, dk_part, dv_part, cand_dq, cand_dk, cand_dv, right, loss = pl.pallas_call(
        main_kernel,
        out_shape=(
            prompt_shape,
            prompt_wide,
            prompt_wide,
            cand_shape,
            cand_shape,
            cand_shape,
            jax.ShapeDtypeStruct((PIECES, LOCAL_HEADS, E, E), BF),
            jax.ShapeDtypeStruct((1, 1), F32),
        ),
        in_specs=[SMEM_SPEC] * 5 + [VMEM_SPEC] + [any_spec] * 7,
        out_specs=[any_spec] * 6 + [VMEM_SPEC] * 2,
        scratch_shapes=[prompt_buf] * 4
        + [cand_buf] * 3
        + [pltpu.VMEM((PIECES, width, E), BF)]
        + [prompt_acc] * 3
        + [prompt_buf]
        + [cand_buf] * 3
        + [
            half_rows(PIECES + 1, HALF, kind=F32),
            half_rows(HALF, PIECES + 1, kind=F32),
            half_rows(HALF, PIECES, kind=F32),
            half_rows(HALF, kind=F32),
            half_rows(HALF, kind=F32),
            half_rows(HALF, kind=F32),
            half_rows(2, LOCAL_HEADS),
            half_rows(HALF, 2),
            half_rows(HALF, 2),
            half_rows(HALF),
            half_rows(HALF),
            half_rows(LOCAL_HEADS),
            half_rows(HALF, kind=F32),
            half_rows(CHIP_ROWS, HALF, kind=F32),
            half_rows(PIECES, HALF),
            half_rows(PIECES, HALF),
            pltpu.VMEM((LOCAL_HEADS, cand_width, cand_width), BF),
            pltpu.VMEM((LOCAL_HEADS, cand_width, E), F32),
            pltpu.VMEM((LOCAL_HEADS, cand_width, E), BF),
            half_rows(HALF, 2),
            pltpu.VMEM((1, E), F32),
            pltpu.VMEM((4, 1, E), F32),
            pltpu.VMEM((1, E), F32),
            pltpu.VMEM((slabs, 1, E), F32),
            half_rows(RING, HALF, CHIP_ENDS),
            half_rows(RING, HALF, 3, kind=F32),
            half_rows(RING, HALF, kind=F32),
            half_rows(RING, HALF, NONE + 1),
            pltpu.VMEM((4, slabs, E), jnp.int32),
            dma((7,)),
            dma((6,)),
            dma((7,)),
            dma((7,)),
            dma((4, 6)),
            dma((4, 6)),
            dma((3,)),
            dma((3,)),
            dma((slabs,)),
            dma((slabs,)),
        ]
        + Spread.scratch(4, F32)
        + Spread.scratch(2, F32)
        + Spread.scratch(CHIP_ROWS, BF),
        compiler_params=pltpu.CompilerParams(
            collective_id=0, has_side_effects=True, vmem_limit_bytes=56 << 20
        ),
        name="exchange",
    )(
        meta,
        prompt_ends,
        cand_prompt,
        cand_lengths,
        cand_ranks,
        readout.reshape(1, flat),
        prompt_q,
        prompt_k,
        prompt_v,
        prompt_grad,
        cand_q,
        cand_k,
        cand_v,
    )

    prompt_block = pl.BlockSpec((width, E), lambda h: (0, h))
    cand_block = pl.BlockSpec((cand_width, E), lambda h: (0, h))
    prompt_dq, prompt_dk, prompt_dv, cand_dq, cand_dk, cand_dv = pl.pallas_call(
        last_kernel,
        grid=(LOCAL_HEADS,),
        out_shape=(prompt_shape,) * 3 + (cand_shape,) * 3,
        in_specs=[SMEM_SPEC] * 2
        + [prompt_block] * 4
        + [pl.BlockSpec((PIECES, 1, E, E), lambda h: (0, h, 0, 0)), prompt_block]
        + [cand_block] * 3,
        out_specs=(prompt_block,) * 3 + (cand_block,) * 3,
        name="finish",
    )(
        meta,
        prompt_ends,
        prompt_k,
        prompt_v,
        dk_part,
        dv_part,
        right,
        dq_part,
        cand_dq,
        cand_dk,
        cand_dv,
    )
    return (
        prompt_dq,
        prompt_dk,
        prompt_dv,
        cand_dq,
        cand_dk,
        cand_dv,
        loss.reshape(()),
    )


def solution(mesh):
    both = P("seq", "head")
    return jax.shard_map(
        per_device,
        mesh=mesh,
        in_specs=(
            both,
            both,
            both,
            both,
            both,
            both,
            both,
            P("head"),
            P(),
            P("seq", None),
            P(),
            P(),
        ),
        out_specs=(both, both, both, both, both, both, P()),
        check_vma=False,
    )
```

```python
import functools
import math

import jax
import jax.numpy as jnp
from jax import lax
from jax.experimental import pallas as pl
from jax.experimental.pallas import tpu as pltpu
from jax.sharding import PartitionSpec as P

E = 128
LOCAL_HEADS = 4
HALF = LOCAL_HEADS // 2
RING = 4
CHUNK = 256
PIECES = 3
CHIP_ROWS = 5
CHIP_ENDS = 4
SUM01, SUM23, NONE = 4, 5, 6
FAR = 1 << 30
GRAD_SCALE = 1048576.0
MESH = pl.DeviceIdType.MESH
BF = jnp.bfloat16
F32 = jnp.float32

VMEM_SPEC = pl.BlockSpec(memory_space=pltpu.VMEM)
SMEM_SPEC = pl.BlockSpec(memory_space=pltpu.SMEM)


def dot_nn(a, b):
    return lax.dot_general(a, b, (((1,), (0,)), ((), ())), preferred_element_type=F32)


def dot_nt(a, b):
    return lax.dot_general(a, b, (((1,), (1,)), ((), ())), preferred_element_type=F32)


def dot_tn(a, b):
    return lax.dot_general(a, b, (((0,), (0,)), ((), ())), preferred_element_type=F32)


def counts_of(ends_ref, marks):
    def one(at, held):
        end = ends_ref[at]
        return tuple(count + (end <= mark).astype(jnp.int32) for count, mark in zip(held, marks))

    zero = jnp.int32(0)
    return lax.fori_loop(0, ends_ref.shape[0], one, (zero,) * len(marks), unroll=True)


def local_ends(first, ends_ref, slab, width):
    last = ends_ref.shape[0] - 1
    end0 = ends_ref[jnp.minimum(first, last)] - slab * width
    end1 = jnp.where(
        first + 1 <= last, ends_ref[jnp.minimum(first + 1, last)] - slab * width, FAR
    )
    return end0, end1


class Place:
    def __init__(self):
        self.seq = lax.axis_index("seq")
        self.head = lax.axis_index("head")
        self.core = self.seq % 2
        x = (self.seq // 2) % RING
        z = self.seq // (2 * RING)
        self.pos_a = z * (1 - self.core) + x * self.core
        self.pos_b = x * (1 - self.core) + z * self.core
        self.step_a = 8 - 6 * self.core
        self.step_b = 2 + 6 * self.core

    def chip_at(self, move_a, move_b):
        return ((self.pos_a + move_a) % RING) * self.step_a + (
            (self.pos_b + move_b) % RING
        ) * self.step_b

    def neighbour(self, move_a, move_b):
        return (self.chip_at(move_a, move_b) + self.core, self.head)

    def partner(self):
        return (self.seq + 1 - 2 * self.core, self.head)


class Spread:
    COPIES = 6

    @staticmethod
    def scratch(rows, kind):
        return [
            pltpu.VMEM((RING, HALF, rows, E, E), kind),
            pltpu.VMEM((2, rows, E, E), F32),
            pltpu.VMEM((HALF, rows, E, E), kind),
            pltpu.VMEM((2, HALF, rows, E, E), kind),
            pltpu.SemaphoreType.DMA((Spread.COPIES,)),
            pltpu.SemaphoreType.DMA((Spread.COPIES,)),
        ]

    def __init__(self, place, rows, scratch, term):
        self.rows, self.term = rows, term
        self.parts, self.exact, self.passed, self.arrived, send, recv = scratch
        left, right = place.neighbour(0, RING - 1), place.neighbour(0, 1)
        parts, passed, arrived = self.parts, self.passed, self.arrived
        pairs = (
            (parts.at[2, 0], passed.at[0], left),
            (parts.at[2, 1], passed.at[1], right),
            (parts.at[3, 1], arrived.at[0, 1], left),
            (parts.at[1, 0], arrived.at[1, 0], right),
            (parts.at[3, 0], arrived.at[0, 0], left),
            (parts.at[1, 1], arrived.at[1, 1], right),
        )
        self.copies = [
            remote_copy(src, dst, send.at[at], recv.at[at], device)
            for at, (src, dst, device) in enumerate(pairs)
        ]

    def begin(self):
        for at, (m, i) in enumerate(((2, 0), (2, 1), (3, 1), (1, 0))):
            for r in range(self.rows):
                self.parts[m, i, r] = self.term(m, i, r).astype(self.parts.dtype)
            self.copies[at].start()

    def pass_on(self):
        for at, (m, i) in enumerate(((3, 0), (1, 1))):
            for r in range(self.rows):
                self.exact[at, r] = self.term(m, i, r).astype(F32)
        for at, (m, i) in enumerate(((3, 0), (1, 1))):
            self.copies[at].wait_recv()
            for r in range(self.rows):
                self.parts[m, i, r] = (
                    self.exact[at, r] + self.passed[i, r].astype(F32)
                ).astype(self.parts.dtype)
            self.copies[4 + at].start()

    def arrive(self):
        for copy in self.copies[2:]:
            copy.wait_recv()

    def result(self, i, r):
        return (
            self.term(0, i, r).astype(F32)
            + self.arrived[0, i, r].astype(F32)
            + self.arrived[1, i, r].astype(F32)
        )

    def finish(self):
        for copy in self.copies:
            copy.wait_send()


class SplitSpread(Spread):
    LEGS = 4

    @staticmethod
    def scratch(rows, kind):
        each = rows // 2
        return [
            pltpu.VMEM((RING, HALF, rows, E, E), kind),
            pltpu.VMEM((2, rows, E, E), F32),
            pltpu.VMEM((HALF, rows, E, E), kind),
            pltpu.VMEM((2, 2, HALF, each, E, E), kind),
            pltpu.VMEM((HALF, each, E, E), kind),
            pltpu.VMEM((HALF, each, E, E), kind),
            pltpu.SemaphoreType.DMA((3,)),
            pltpu.SemaphoreType.DMA((3,)),
            pltpu.SemaphoreType.DMA((SplitSpread.LEGS, 2)),
            pltpu.SemaphoreType.DMA((SplitSpread.LEGS, 2)),
        ]

    def __init__(self, place, rows, scratch, term):
        self.rows, self.term, self.place = rows, term, place
        self.parts, self.exact, self.passed, self.arrived, self.mail, self.mailed = scratch[:6]
        send, recv, leg_send, leg_recv = scratch[6:]
        left, right = place.neighbour(0, RING - 1), place.neighbour(0, 1)
        each = rows // 2
        self.far = [
            remote_copy(self.parts.at[2, 0], self.passed.at[0], send.at[0], recv.at[0], left),
            remote_copy(self.parts.at[2, 1], self.passed.at[1], send.at[1], recv.at[1], right),
        ]
        self.swap = remote_copy(self.mail, self.mailed, send.at[2], recv.at[2], place.partner())
        self.legs, self.awaited = [], []
        for leg, (m, i, side) in enumerate(((3, 1, 0), (1, 0, 1), (3, 0, 0), (1, 1, 1))):
            chip = place.chip_at(0, m)
            self.legs.append([])
            for cd in range(2):
                src = self.parts.at[m, i, pl.ds(each * cd, each)]
                self.legs[-1].append(
                    remote_copy(
                        src,
                        self.arrived.at[place.core, side, i],
                        leg_send.at[leg, cd],
                        leg_recv.at[leg, place.core],
                        (chip + cd, place.head),
                    )
                )
                self.awaited.append(
                    remote_copy(
                        src,
                        self.arrived.at[cd, side, i],
                        leg_send.at[leg, cd],
                        leg_recv.at[leg, cd],
                        (chip + cd, place.head),
                    )
                )

    def begin(self):
        for at, (m, i) in enumerate(((2, 0), (2, 1), (3, 1), (1, 0))):
            for r in range(self.rows):
                self.parts[m, i, r] = self.term(m, i, r).astype(self.parts.dtype)
            for copy in self.far[at : at + 1] if at < 2 else self.legs[at - 2]:
                copy.start()
        each = self.rows // 2
        for i in range(HALF):
            for r in range(each):
                self.mail[i, r] = self.term(0, i, each * (1 - self.place.core) + r)
        self.swap.start()

    def pass_on(self):
        for at, (m, i) in enumerate(((3, 0), (1, 1))):
            for r in range(self.rows):
                self.exact[at, r] = self.term(m, i, r).astype(F32)
        for at, (m, i) in enumerate(((3, 0), (1, 1))):
            self.far[at].wait_recv()
            for r in range(self.rows):
                self.parts[m, i, r] = (
                    self.exact[at, r] + self.passed[i, r].astype(F32)
                ).astype(self.parts.dtype)
            for copy in self.legs[2 + at]:
                copy.start()

    def arrive(self):
        self.swap.wait_recv()
        for copy in self.awaited:
            copy.wait_recv()

    def result(self, i, r, own):
        each = self.rows // 2
        core = self.place.core
        side = core if own else 1 - core
        base = self.term(0, i, each * core + r) if own else self.mailed[i, r]
        return base + self.arrived[side, 0, i, r] + self.arrived[side, 1, i, r]

    def finish(self):
        for copy in self.far + [self.swap] + self.legs[0] + self.legs[1] + self.legs[2] + self.legs[3]:
            copy.wait_send()


class Gather:
    COPIES = 6

    def __init__(self, place, block, send, recv):
        left, right = place.neighbour(RING - 1, 0), place.neighbour(1, 0)
        pairs = (
            (block(0, 0), block(1, 0), left),
            (block(0, 1), block(3, 1), right),
            (block(0, 1), block(1, 1), left),
            (block(0, 0), block(3, 0), right),
            (block(1, 0), block(2, 0), left),
            (block(3, 1), block(2, 1), right),
        )
        self.copies = [
            remote_copy(src, dst, send.at[at], recv.at[at], device)
            for at, (src, dst, device) in enumerate(pairs)
        ]

    def begin(self):
        for copy in self.copies[:4]:
            copy.start()

    def pass_on(self):
        for at in range(2):
            self.copies[at].wait_recv()
            self.copies[4 + at].start()

    def arrive(self):
        for copy in self.copies[2:]:
            copy.wait_recv()
        for copy in self.copies:
            copy.wait_send()


def remote_copy(src, dst, send, recv, device):
    return pltpu.make_async_remote_copy(
        src_ref=src,
        dst_ref=dst,
        send_sem=send,
        recv_sem=recv,
        device_id=device,
        device_id_type=MESH,
    )


def flag(condition):
    return jnp.where(condition, 1.0, 0.0).astype(F32)


def lanes(head):
    return pl.ds(pl.multiple_of(head * E, E), E)


def main_kernel(
    ends_ref,
    cand_ref,
    lens_ref,
    ranks_ref,
    readout_ref,
    pq_hbm,
    pk_hbm,
    pv_hbm,
    pg_hbm,
    cq_hbm,
    ck_hbm,
    cv_hbm,
    dq_hbm,
    dkp_hbm,
    dvp_hbm,
    cdq_hbm,
    cdk_hbm,
    cdv_hbm,
    right_ref,
    loss_ref,
    pq,
    pk,
    pv,
    pg,
    cq,
    ck,
    cv,
    masks,
    dq_acc,
    dkp,
    dvp,
    dq_out,
    cdq,
    cdk,
    cdv,
    own,
    theirs,
    mail,
    qg_own,
    qg_theirs,
    qg_mail,
    states,
    carry_mail,
    carry_in,
    carry,
    chip_carry,
    right_sum,
    right_mail,
    right_in,
    attn_ref,
    outs_ref,
    dout_ref,
    grads_mail,
    mine_ref,
    heads_ref,
    total_ref,
    scores_ref,
    gathered,
    gathered_wide,
    gathered_qg,
    gathered_grads,
    table_ref,
    firsts_ref,
    lasts_ref,
    dk_out,
    dv_out,
    in_sem,
    out_sem,
    swap_send,
    swap_recv,
    ring_send,
    ring_recv,
    y_send,
    y_recv,
    s_send,
    s_recv,
    *spread_scratch,
):
    place = Place()
    core = place.core
    slabs = lax.axis_size("seq")
    planes = lax.axis_size("head")
    width = pq.shape[0]
    cand_width = cq.shape[0]
    scaling = 1.0 / math.sqrt(E * width)
    barrier = pltpu.get_barrier_semaphore()

    def other_slab(at):
        return (place.seq + at) % slabs, place.head

    def hello(at, held):
        pl.semaphore_signal(barrier, inc=1, device_id=other_slab(at), device_id_type=MESH)
        return held

    loads = [
        pltpu.make_async_copy(src, dst, in_sem.at[at])
        for at, (src, dst) in enumerate(
            (
                (pk_hbm, pk),
                (pv_hbm, pv),
                (pg_hbm, pg),
                (pq_hbm, pq),
                (cq_hbm, cq),
                (ck_hbm, ck),
                (cv_hbm, cv),
            )
        )
    ]
    loads[0].start()
    loads[1].start()
    lax.fori_loop(slabs // 2, slabs, hello, 0)
    lax.fori_loop(1, slabs // 2, hello, 0)
    planes_other = [(place.seq, (place.head + at) % planes) for at in range(1, planes)]
    for device in planes_other:
        pl.semaphore_signal(barrier, inc=1, device_id=device, device_id_type=MESH)

    def store(at, src, dst):
        copy = pltpu.make_async_copy(src, dst, out_sem.at[at])
        copy.start()
        return copy

    def swap(at, src, dst):
        return remote_copy(src, dst, swap_send.at[at], swap_recv.at[at], place.partner())

    chip = place.chip_at(0, 0)
    seam_at = (chip + 1) * width
    first0, last0, first1, last1 = counts_of(
        ends_ref, (chip * width, seam_at - 1, seam_at, seam_at + width - 1)
    )
    end0, end1 = local_ends(
        jnp.where(core == 0, first0, first1), ends_ref, place.seq, width
    )
    spot = lax.broadcasted_iota(jnp.int32, (width, E), 0)
    masks[0] = flag(spot < end0).astype(BF)
    masks[1] = flag(jnp.logical_and(spot >= end0, spot < end1)).astype(BF)
    masks[2] = flag(spot >= end1).astype(BF)

    def piece_sums(head):
        v = pv[:, lanes(head)]
        split = jnp.concatenate([v * masks[j] for j in range(PIECES)], axis=1)
        return dot_tn(pk[:, lanes(head)], split)

    loads[0].wait()
    loads[1].wait()
    for load in loads[2:]:
        load.start()
    pieces_swaps = []
    for i in range(HALF):
        sums = piece_sums(HALF * (1 - core) + i)
        for j in range(PIECES):
            mail[i, j] = sums[:, j * E : (j + 1) * E]
        pieces_swaps.append(swap(6 * i, mail.at[i], theirs.at[i, pl.ds(0, PIECES)]))
    pl.semaphore_wait(barrier, slabs - 1 + planes - 1)
    for copy in pieces_swaps:
        copy.start()
    for i in range(HALF):
        sums = piece_sums(HALF * core + i)
        for j in range(PIECES):
            own[j, i] = sums[:, j * E : (j + 1) * E]
        own[PIECES, i] = jnp.zeros((E, E), F32)
        theirs[i, PIECES] = jnp.zeros((E, E), F32)
        for k in range(RING):
            gathered[k, i, CHIP_ENDS - 1] = jnp.zeros((E, E), BF)
            gathered_wide[k, i, 2] = jnp.zeros((E, E), F32)
            gathered_grads[k, i, NONE] = jnp.zeros((E, E), BF)

    off = jnp.clip(first1 - first0, 0, PIECES - 1)
    off_own, off_theirs = off * core, off * (1 - core)

    def slot_in(j, count):
        return jnp.where(jnp.logical_and(j >= 0, j < count), j, count)

    def chip_row(i, j):
        at_own, at_theirs = slot_in(j - off_own, PIECES), slot_in(j - off_theirs, PIECES)
        return own[at_own, i] + theirs[i, at_theirs]

    tail0 = jnp.where(last0 == last1, slot_in(last0 - first0, PIECES), PIECES)
    tail1 = slot_in(last1 - first1, PIECES)
    tail_own = jnp.where(core == 0, tail0, tail1)
    tail_theirs = jnp.where(core == 0, tail1, tail0)
    wide_ring = Gather(
        place,
        lambda k, i: gathered_wide.at[k, i, pl.ds(0, 2)],
        ring_send.at[0],
        ring_recv.at[0],
    )
    ends_ring = Gather(
        place,
        lambda k, i: gathered.at[k, i, pl.ds(0, CHIP_ENDS - 1)],
        ring_send.at[1],
        ring_recv.at[1],
    )
    for copy in pieces_swaps:
        copy.wait()
    for i in range(HALF):
        gathered_wide[0, i, 0] = chip_row(i, 0)
        gathered_wide[0, i, 1] = own[tail_own, i] + theirs[i, tail_theirs]
    wide_ring.begin()
    for i in range(HALF):
        for j in range(1, CHIP_ENDS):
            gathered[0, i, j - 1] = chip_row(i, j).astype(BF)
    ends_ring.begin()

    def count_chip(at, held):
        start = at * 2 * width
        firsts_ref[at], lasts_ref[at] = counts_of(ends_ref, (start, start + 2 * width - 1))
        return held

    lax.fori_loop(0, slabs // 2, count_chip, 0)

    def first_of(seq):
        return firsts_ref[seq // 2]

    def last_of(seq):
        return lasts_ref[seq // 2]

    def segment_of(at):
        return (at >= end0).astype(jnp.int32) + (at >= end1).astype(jnp.int32)

    def prompt_task(at, low, high):
        rows = slice(at * CHUNK, (at + 1) * CHUNK)
        span = (at + 1) * CHUNK
        i = lax.broadcasted_iota(jnp.int32, (CHUNK, 1), 0) + at * CHUNK
        j = lax.broadcasted_iota(jnp.int32, (1, span), 1)
        same = jnp.logical_and(segment_of(i) == segment_of(j), j <= i)

        def one(h, held):
            cols = lanes(h)
            q, g = pq[rows, cols], pg[rows, cols]
            attn = jnp.where(same, dot_nt(q, pk[:span, cols]), 0.0).astype(BF)
            weights = jnp.where(same, dot_nt(g, pv[:span, cols]), 0.0).astype(BF)
            dq_acc[rows, cols] = dot_nn(weights, pk[:span, cols])
            dk = scaling * dot_tn(weights, q)
            dv = scaling * dot_tn(attn, g)
            if span == width:
                dkp[:, cols] = dk
                dvp[:, cols] = dv
            else:
                dkp[:span, cols] += dk
                dvp[:span, cols] += dv
            return held

        lax.fori_loop(low, high, one, 0)

    len0 = lens_ref[0, 0]
    len1 = lens_ref[0, 1]
    in_second = lax.broadcasted_iota(jnp.int32, (cand_width, 1), 0) >= len0

    def same_cand():
        i = lax.broadcasted_iota(jnp.int32, (cand_width, 1), 0)
        j = lax.broadcasted_iota(jnp.int32, (1, cand_width), 1)
        return jnp.logical_and(j <= i, (i >= len0).astype(jnp.int32) == (j >= len0).astype(jnp.int32))

    def cand_near(low, high):
        if low == 0:
            for load in loads[4:]:
                load.wait()

        def one(h, held):
            cols = lanes(h)
            attn = jnp.where(same_cand(), dot_nt(cq[:, cols], ck[:, cols]), 0.0).astype(BF)
            attn_ref[h] = attn
            outs_ref[h] = dot_nn(attn, cv[:, cols])
            return held

        lax.fori_loop(low, high, one, 0)

    def cand_backward(low, high):
        def one(h, held):
            cols = lanes(h)
            dout = dout_ref[h]
            weights = jnp.where(same_cand(), dot_nt(dout, cv[:, cols]), 0.0).astype(BF)
            far = jnp.where(in_second, dot_nt(dout, states[1, h]), dot_nt(dout, states[0, h]))
            cdq[:, cols] = (scaling * (dot_nn(weights, ck[:, cols]) + far)).astype(BF)
            cdk[:, cols] = (scaling * dot_tn(weights, cq[:, cols])).astype(BF)
            cdv[:, cols] = (scaling * dot_tn(attn_ref[h], dout)).astype(BF)
            return held

        lax.fori_loop(low, high, one, 0)

    def dq_finish():
        def one(h, held):
            cols = lanes(h)
            far = dot_nt(pg[:, cols], carry[h])
            inside = lax.broadcasted_iota(jnp.int32, (width, 1), 0) < end0
            dq_out[:, cols] = (scaling * (dq_acc[:, cols] + jnp.where(inside, far, 0.0))).astype(BF)
            return held

        lax.fori_loop(0, LOCAL_HEADS, one, 0)

    loads[2].wait()
    loads[3].wait()

    def qg_sum(head):
        return scaling * dot_tn(pq[:, lanes(head)], pg[:, lanes(head)] * masks[0])

    for i in range(HALF):
        qg_mail[i] = qg_sum(HALF * (1 - core) + i)
    qg_swap = swap(1, qg_mail, qg_theirs)
    qg_swap.start()
    for i in range(HALF):
        qg_own[i] = qg_sum(HALF * core + i)
    wide_ring.pass_on()
    ends_ring.pass_on()
    prompt_task(3, 0, 3)
    whole = flag(off == 0)

    def carry_term(m, i):
        dest = place.chip_at(0, m)
        total = None
        for k in range(RING):
            src = place.chip_at(k, 0)
            same = jnp.logical_and(last_of(src) == first_of(dest), src < dest)
            term = gathered_wide[k, i, jnp.where(same, 1, 2)]
            total = term if total is None else total + term
        return total

    def memory_term(m, i, r):
        if r == 0:
            return carry_term(m, i)
        dest = place.chip_at(0, m)
        total = None
        for k in range(RING):
            src = place.chip_at(k, 0)
            same = jnp.logical_and(first_of(src) == last_of(dest), src > dest)
            term = flag(same) * gathered_qg[k, i]
            total = term if total is None else total + term
        return total

    def state_term(m, i, r):
        wanted = cand_ref[2 * place.chip_at(0, m) + r]
        source = jnp.clip((ends_ref[wanted] - 1) // (2 * width), 0, slabs // 2 - 1)
        src_z, src_x = source // RING, source % RING
        src_a = jnp.where(core == 0, src_z, src_x)
        src_b = jnp.where(core == 0, src_x, src_z)
        k_end = (src_a - place.pos_a + RING) % RING
        row = wanted - first_of(2 * source)
        inner = jnp.logical_and(src_b == place.pos_b, row > 0)
        total = gathered[k_end, i, jnp.where(inner, jnp.minimum(row - 1, CHIP_ENDS - 2), CHIP_ENDS - 1)].astype(F32)
        for k in range(RING):
            src = place.chip_at(k, 0)
            opens = jnp.logical_and(src < 2 * source, last_of(src) == wanted)
            ends = jnp.logical_and(src == 2 * source, row == 0)
            total = total + gathered_wide[k, i, jnp.where(opens, 1, jnp.where(ends, 0, 2))]
        return total

    def grad_term(m, i, r):
        wanted = first_of(place.chip_at(0, m)) + r
        total = None
        for k in range(RING):
            src = 2 * place.chip_at(k, 0)
            is0, is1, is2, is3 = [cand_ref[src + c] == wanted for c in range(4)]
            slot0 = jnp.where(is0, jnp.where(is1, SUM01, 0), jnp.where(is1, 1, NONE))
            slot1 = jnp.where(is2, jnp.where(is3, SUM23, 2), jnp.where(is3, 3, NONE))
            term = gathered_grads[k, i, slot0].astype(F32) + gathered_grads[k, i, slot1].astype(F32)
            total = term if total is None else total + term
        return total

    to_states = SplitSpread(place, 4, spread_scratch[:10], state_term)
    to_memory = Spread(place, 2, spread_scratch[10:16], memory_term)
    to_grads = Spread(place, CHIP_ROWS, spread_scratch[16:], grad_term)

    qg_swap.wait()
    own_scale = jnp.where(core == 0, 1.0, whole)
    their_scale = jnp.where(core == 0, whole, 1.0)
    for i in range(HALF):
        gathered_qg[0, i] = own_scale * qg_own[i] + their_scale * qg_theirs[i]
    qg_ring = Gather(place, lambda k, i: gathered_qg.at[k, i], ring_send.at[2], ring_recv.at[2])
    wide_ring.arrive()
    ends_ring.arrive()
    qg_ring.begin()
    to_states.begin()
    cand_near(0, 2)
    to_states.pass_on()
    qg_ring.pass_on()
    cand_near(2, 4)
    prompt_task(3, 3, 4)
    to_states.arrive()
    for i in range(HALF):
        for r in range(2):
            states[r, HALF * core + i] = to_states.result(i, r, True).astype(BF)
            states[r, HALF * (1 - core) + i] = to_states.result(i, r, False).astype(BF)

    sum_all = jnp.zeros((1, E), F32)
    sum_second = jnp.zeros((1, E), F32)
    for h in range(LOCAL_HEADS):
        cols = slice(h * E, (h + 1) * E)
        far = jnp.where(
            in_second, dot_nn(cq[:, cols], states[1, h]), dot_nn(cq[:, cols], states[0, h])
        )
        out = scaling * (outs_ref[h] + far)
        outs_ref[h] = out
        part = out / (1.0 + jnp.exp(-out)) * readout_ref[:, cols]
        sum_all = sum_all + jnp.sum(part, axis=0, keepdims=True)
        sum_second = sum_second + jnp.sum(jnp.where(in_second, part, 0.0), axis=0, keepdims=True)
    second = jnp.sum(sum_second, axis=1, keepdims=True)
    first = jnp.sum(sum_all - sum_second, axis=1, keepdims=True)
    lane = lax.broadcasted_iota(jnp.int32, (1, E), 1)
    mine_ref[...] = jnp.where(
        lane == 0,
        first / len0.astype(F32),
        jnp.where(lane == 1, second / len1.astype(F32), 0.0),
    )
    to_planes = [
        remote_copy(mine_ref, heads_ref.at[place.head], y_send.at[at], y_recv.at[at], device)
        for at, device in enumerate(planes_other)
    ]
    for copy in to_planes:
        copy.start()
    heads_ref[place.head] = mine_ref[...]
    qg_ring.arrive()
    to_memory.begin()
    prompt_task(2, 0, 2)
    for copy in to_planes:
        copy.wait()
    total = heads_ref[0]
    for at in range(1, planes):
        total = total + heads_ref[at]
    total_ref[...] = total

    def score_copy(at):
        return remote_copy(
            total_ref, scores_ref.at[place.seq], s_send.at[at], s_recv.at[at], other_slab(at)
        )

    def tell(at, held):
        score_copy(at).start()
        return held

    def told(at, held):
        score_copy(at).wait()
        return held

    def build_table():
        rows = lax.broadcasted_iota(jnp.int32, (slabs, E), 0)

        def one(at, held):
            here = rows == at
            values = (
                cand_ref[2 * at],
                cand_ref[2 * at + 1],
                ranks_ref[2 * at],
                ranks_ref[2 * at + 1],
            )
            return tuple(jnp.where(here, value, old) for value, old in zip(values, held))

        blank = jnp.zeros((slabs, E), jnp.int32)
        for at, plane in enumerate(lax.fori_loop(0, slabs, one, (blank,) * 4)):
            table_ref[at] = plane

    lax.fori_loop(slabs // 2, slabs, tell, 0)
    lax.fori_loop(1, slabs // 2, tell, 0)
    scores_ref[place.seq] = total
    build_table()
    to_memory.pass_on()
    prompt_task(2, 2, 4)
    lax.fori_loop(1, slabs, told, 0)

    raw = scores_ref[...].reshape(slabs, E)
    prompts = lax.broadcasted_iota(jnp.int32, (slabs, E), 1)
    tanh_raw = jnp.tanh(raw)
    squashed = 3.0 * tanh_raw
    exp_scores = jnp.exp(squashed)
    hot = [(table_ref[j] == prompts).astype(F32) for j in range(2)]
    weight = [jnp.exp(-table_ref[2 + j].astype(F32)) for j in range(2)]
    group_exp = jnp.sum(
        hot[0] * exp_scores[:, 0:1] + hot[1] * exp_scores[:, 1:2], axis=0, keepdims=True
    )
    group_weight = jnp.sum(hot[0] * weight[0] + hot[1] * weight[1], axis=0, keepdims=True)
    own_row = lax.broadcasted_iota(jnp.int32, (slabs, 1), 0) == place.seq
    loss = jnp.zeros((1, 1), F32)
    coefs = []
    for j in range(2):
        denom = jnp.sum(hot[j] * group_exp, axis=1, keepdims=True)
        target = weight[j][:, 0:1] / jnp.sum(hot[j] * group_weight, axis=1, keepdims=True)
        score = squashed[:, j : j + 1]
        loss = loss + jnp.sum(target * (score - jnp.log(denom)), axis=0, keepdims=True)
        tanh_j = tanh_raw[:, j : j + 1]
        grad = (
            GRAD_SCALE
            / slabs
            * (exp_scores[:, j : j + 1] / denom - target)
            * 3.0
            * (1.0 - tanh_j * tanh_j)
        )
        coefs.append(jnp.sum(jnp.where(own_row, grad, 0.0), axis=0, keepdims=True))
    loss_ref[...] = -loss / slabs
    coef = jnp.where(in_second, coefs[1] / len1.astype(F32), coefs[0] / len0.astype(F32))

    def grad_sums(h):
        out = outs_ref[h]
        sigma = 1.0 / (1.0 + jnp.exp(-out))
        slope = coef * readout_ref[:, lanes(h)] * sigma * (1.0 + out * (1.0 - sigma))
        dout_ref[h] = slope.astype(BF)
        split = jnp.concatenate(
            [
                jnp.where(in_second, 0.0, slope).astype(BF),
                jnp.where(in_second, slope, 0.0).astype(BF),
            ],
            axis=1,
        )
        return scaling * dot_tn(cq[:, lanes(h)], split)

    for i in range(HALF):
        sums = grad_sums(HALF * (1 - core) + i)
        for r in range(2):
            grads_mail[i, r] = sums[:, r * E : (r + 1) * E].astype(BF)
    own_slots = pl.ds(2 * core, 2)
    grads_swap = swap(3, grads_mail, gathered_grads.at[0, :, own_slots])
    grads_swap.start()
    for i in range(HALF):
        sums = grad_sums(HALF * core + i)
        for r in range(2):
            gathered_grads[0, i, 2 * core + r] = sums[:, r * E : (r + 1) * E].astype(BF)
    grads_swap.wait()
    grads_ring = Gather(
        place,
        lambda k, i: gathered_grads.at[k, i, pl.ds(0, 4)],
        ring_send.at[3],
        ring_recv.at[3],
    )
    grads_ring.begin()

    to_memory.arrive()
    seam = slot_in(off, PIECES)

    def carry_row(i, at_core):
        before = jnp.where(core == 0, own[seam, i], theirs[i, seam])
        is_second = flag(at_core == 1)
        keep = jnp.where(at_core == 0, 1.0, whole)
        return (keep * chip_carry[i] + is_second * before).astype(BF)

    for i in range(HALF):
        chip_carry[i] = to_memory.result(i, 0)
        carry_mail[i] = carry_row(i, 1 - core)
    carry_swap = swap(4, carry_mail, carry_in)
    carry_swap.start()
    for i in range(HALF):
        carry[HALF * core + i] = carry_row(i, core)
    cand_backward(0, 2)
    grads_ring.pass_on()
    cand_backward(2, 4)
    prompt_task(1, 0, 2)
    outputs = [store(0, cdq, cdq_hbm), store(1, cdk, cdk_hbm), store(2, cdv, cdv_hbm)]
    carry_swap.wait()
    for i in range(HALF):
        carry[HALF * (1 - core) + i] = carry_in[i]
    grads_ring.arrive()
    for k in range(RING):
        for i in range(HALF):
            for target, source in ((SUM01, 0), (SUM23, 2)):
                gathered_grads[k, i, target] = (
                    gathered_grads[k, i, source].astype(F32)
                    + gathered_grads[k, i, source + 1].astype(F32)
                ).astype(BF)
    to_grads.begin()
    prompt_task(1, 2, 4)
    to_grads.pass_on()
    prompt_task(0, 0, 4)
    dk_out[...] = dkp[...].astype(BF)
    dv_out[...] = dvp[...].astype(BF)
    outputs += [store(3, dk_out, dkp_hbm), store(4, dv_out, dvp_hbm)]
    dq_finish()
    outputs.append(store(5, dq_out, dq_hbm))
    to_grads.arrive()
    for i in range(HALF):
        for r in range(CHIP_ROWS):
            right_sum[r, i] = to_grads.result(i, r)

    def later_row(i, at_core):
        chip_later = to_memory.result(i, 1)
        second_qg = jnp.where(core == 0, qg_theirs[i], qg_own[i])
        inner = flag(first1 == last0) * second_qg + flag(last1 == last0) * chip_later
        return jnp.where(at_core == 0, inner, chip_later)

    def right_row(i, j, at_core, later):
        into = jnp.where(at_core == 0, last0 - first0, last1 - first1)
        return (right_sum[j + off * at_core, i] + flag(into == j) * later).astype(BF)

    for i in range(HALF):
        later = later_row(i, 1 - core)
        for j in range(PIECES):
            right_mail[j, i] = right_row(i, j, 1 - core, later)
    right_swap = swap(5, right_mail, right_in)
    right_swap.start()
    for i in range(HALF):
        later = later_row(i, core)
        for j in range(PIECES):
            right_ref[j, HALF * core + i] = right_row(i, j, core, later)
    for spread in (to_states, to_memory, to_grads):
        spread.finish()
    right_swap.wait()
    for i in range(HALF):
        for j in range(PIECES):
            right_ref[j, HALF * (1 - core) + i] = right_in[j, i]
    for copy in outputs:
        copy.wait()


def last_kernel(
    ends_ref,
    k_ref,
    v_ref,
    dkp_ref,
    dvp_ref,
    right_ref,
    dq_in,
    cdq_in,
    cdk_in,
    cdv_in,
    dq_ref,
    dk_ref,
    dv_ref,
    cdq_ref,
    cdk_ref,
    cdv_ref,
):
    width = k_ref.shape[0]
    slab = lax.axis_index("seq")
    first = counts_of(ends_ref, (slab * width,))[0]
    end0, end1 = local_ends(first, ends_ref, slab, width)
    spot = lax.broadcasted_iota(jnp.int32, (width, 1), 0)
    k, v = k_ref[...], v_ref[...]
    dk = [dot_nt(v, right_ref[j, 0]) for j in range(PIECES)]
    dv = [dot_nn(k, right_ref[j, 0]) for j in range(PIECES)]
    for out, part, far in ((dk_ref, dkp_ref, dk), (dv_ref, dvp_ref, dv)):
        chosen = jnp.where(spot < end0, far[0], jnp.where(spot < end1, far[1], far[2]))
        out[...] = (part[...].astype(F32) + chosen).astype(BF)
    dq_ref[...] = dq_in[...]
    cdq_ref[...] = cdq_in[...]
    cdk_ref[...] = cdk_in[...]
    cdv_ref[...] = cdv_in[...]


def per_device(
    prompt_q,
    prompt_k,
    prompt_v,
    prompt_grad,
    cand_q,
    cand_k,
    cand_v,
    readout,
    prompt_ends,
    cand_lengths,
    cand_prompt,
    cand_ranks,
):
    slabs = lax.axis_size("seq")
    width = prompt_q.shape[0]
    cand_width = cand_q.shape[0]
    flat = prompt_q.shape[1]
    any_spec = pl.BlockSpec(memory_space=pl.ANY)
    prompt_shape = jax.ShapeDtypeStruct((width, flat), BF)
    cand_shape = jax.ShapeDtypeStruct((cand_width, flat), BF)
    prompt_buf = pltpu.VMEM((width, flat), BF)
    prompt_acc = pltpu.VMEM((width, flat), F32)
    cand_buf = pltpu.VMEM((cand_width, flat), BF)
    half_rows = lambda *lead, kind=BF: pltpu.VMEM(lead + (E, E), kind)
    dma = pltpu.SemaphoreType.DMA
    dq_part, dk_part, dv_part, cand_dq, cand_dk, cand_dv, right, loss = pl.pallas_call(
        main_kernel,
        out_shape=(
            prompt_shape,
            prompt_shape,
            prompt_shape,
            cand_shape,
            cand_shape,
            cand_shape,
            jax.ShapeDtypeStruct((PIECES, LOCAL_HEADS, E, E), BF),
            jax.ShapeDtypeStruct((1, 1), F32),
        ),
        in_specs=[SMEM_SPEC] * 4 + [VMEM_SPEC] + [any_spec] * 7,
        out_specs=[any_spec] * 6 + [VMEM_SPEC] * 2,
        scratch_shapes=[prompt_buf] * 4
        + [cand_buf] * 3
        + [pltpu.VMEM((PIECES, width, E), BF)]
        + [prompt_acc] * 3
        + [prompt_buf]
        + [cand_buf] * 3
        + [
            half_rows(PIECES + 1, HALF, kind=F32),
            half_rows(HALF, PIECES + 1, kind=F32),
            half_rows(HALF, PIECES, kind=F32),
            half_rows(HALF, kind=F32),
            half_rows(HALF, kind=F32),
            half_rows(HALF, kind=F32),
            half_rows(2, LOCAL_HEADS),
            half_rows(HALF),
            half_rows(HALF),
            half_rows(LOCAL_HEADS),
            half_rows(HALF, kind=F32),
            half_rows(CHIP_ROWS, HALF, kind=F32),
            half_rows(PIECES, HALF),
            half_rows(PIECES, HALF),
            pltpu.VMEM((LOCAL_HEADS, cand_width, cand_width), BF),
            pltpu.VMEM((LOCAL_HEADS, cand_width, E), F32),
            pltpu.VMEM((LOCAL_HEADS, cand_width, E), BF),
            half_rows(HALF, 2),
            pltpu.VMEM((1, E), F32),
            pltpu.VMEM((4, 1, E), F32),
            pltpu.VMEM((1, E), F32),
            pltpu.VMEM((slabs, 1, E), F32),
            half_rows(RING, HALF, CHIP_ENDS),
            half_rows(RING, HALF, 3, kind=F32),
            half_rows(RING, HALF, kind=F32),
            half_rows(RING, HALF, NONE + 1),
            pltpu.VMEM((4, slabs, E), jnp.int32),
            pltpu.SMEM((slabs // 2,), jnp.int32),
            pltpu.SMEM((slabs // 2,), jnp.int32),
            prompt_buf,
            prompt_buf,
            dma((7,)),
            dma((6,)),
            dma((7,)),
            dma((7,)),
            dma((4, 6)),
            dma((4, 6)),
            dma((3,)),
            dma((3,)),
            dma((slabs,)),
            dma((slabs,)),
        ]
        + SplitSpread.scratch(4, F32)
        + Spread.scratch(2, F32)
        + Spread.scratch(CHIP_ROWS, BF),
        compiler_params=pltpu.CompilerParams(
            collective_id=0, has_side_effects=True, vmem_limit_bytes=56 << 20
        ),
        name="exchange",
    )(
        prompt_ends,
        cand_prompt,
        cand_lengths,
        cand_ranks,
        readout.reshape(1, flat),
        prompt_q,
        prompt_k,
        prompt_v,
        prompt_grad,
        cand_q,
        cand_k,
        cand_v,
    )

    prompt_block = pl.BlockSpec((width, E), lambda h: (0, h))
    cand_block = pl.BlockSpec((cand_width, E), lambda h: (0, h))
    prompt_dq, prompt_dk, prompt_dv, cand_dq, cand_dk, cand_dv = pl.pallas_call(
        last_kernel,
        grid=(LOCAL_HEADS,),
        out_shape=(prompt_shape,) * 3 + (cand_shape,) * 3,
        in_specs=[SMEM_SPEC]
        + [prompt_block] * 4
        + [pl.BlockSpec((PIECES, 1, E, E), lambda h: (0, h, 0, 0)), prompt_block]
        + [cand_block] * 3,
        out_specs=(prompt_block,) * 3 + (cand_block,) * 3,
        name="finish",
    )(
        prompt_ends,
        prompt_k,
        prompt_v,
        dk_part,
        dv_part,
        right,
        dq_part,
        cand_dq,
        cand_dk,
        cand_dv,
    )
    return (
        prompt_dq,
        prompt_dk,
        prompt_dv,
        cand_dq,
        cand_dk,
        cand_dv,
        loss.reshape(()),
    )


def solution(mesh):
    both = P("seq", "head")
    return jax.shard_map(
        per_device,
        mesh=mesh,
        in_specs=(
            both,
            both,
            both,
            both,
            both,
            both,
            both,
            P("head"),
            P(),
            P("seq", None),
            P(),
            P(),
        ),
        out_specs=(both, both, both, both, both, both, P()),
        check_vma=False,
    )
```

```python
import functools
import math

import jax
import jax.numpy as jnp
from jax import lax
from jax.experimental import pallas as pl
from jax.experimental.pallas import tpu as pltpu
from jax.sharding import PartitionSpec as P

E = 128
LOCAL_HEADS = 4
HALF = LOCAL_HEADS // 2
RING = 4
CHUNK = 256
PIECES = 3
CHIP_ENDS = 4
SUM01, SUM23, NONE = 4, 5, 6
FAR = 1 << 30
GRAD_SCALE = 1048576.0
MESH = pl.DeviceIdType.MESH
BF = jnp.bfloat16
F32 = jnp.float32

VMEM_SPEC = pl.BlockSpec(memory_space=pltpu.VMEM)
SMEM_SPEC = pl.BlockSpec(memory_space=pltpu.SMEM)


def dot_nn(a, b):
    return lax.dot_general(a, b, (((1,), (0,)), ((), ())), preferred_element_type=F32)


def dot_nt(a, b):
    return lax.dot_general(a, b, (((1,), (1,)), ((), ())), preferred_element_type=F32)


def dot_tn(a, b):
    return lax.dot_general(a, b, (((0,), (0,)), ((), ())), preferred_element_type=F32)


def counts_of(ends_ref, marks):
    def one(at, held):
        end = ends_ref[at]
        return tuple(count + (end <= mark).astype(jnp.int32) for count, mark in zip(held, marks))

    zero = jnp.int32(0)
    return lax.fori_loop(0, ends_ref.shape[0], one, (zero,) * len(marks), unroll=True)


def local_ends(first, ends_ref, slab, width):
    last = ends_ref.shape[0] - 1
    end0 = ends_ref[jnp.minimum(first, last)] - slab * width
    end1 = jnp.where(
        first + 1 <= last, ends_ref[jnp.minimum(first + 1, last)] - slab * width, FAR
    )
    return end0, end1


class Place:
    def __init__(self):
        self.seq = lax.axis_index("seq")
        self.head = lax.axis_index("head")
        self.core = self.seq % 2
        x = (self.seq // 2) % RING
        z = self.seq // (2 * RING)
        self.pos_a = z * (1 - self.core) + x * self.core
        self.pos_b = x * (1 - self.core) + z * self.core
        self.step_a = 8 - 6 * self.core
        self.step_b = 2 + 6 * self.core

    def chip_at(self, move_a, move_b):
        return ((self.pos_a + move_a) % RING) * self.step_a + (
            (self.pos_b + move_b) % RING
        ) * self.step_b

    def neighbour(self, move_a, move_b):
        return (self.chip_at(move_a, move_b) + self.core, self.head)

    def partner(self):
        return (self.seq + 1 - 2 * self.core, self.head)


class Spread:
    COPIES = 6

    @staticmethod
    def scratch(rows, kind):
        return [
            pltpu.VMEM((RING, HALF, rows, E, E), kind),
            pltpu.VMEM((2, rows, E, E), F32),
            pltpu.VMEM((HALF, rows, E, E), kind),
            pltpu.VMEM((2, HALF, rows, E, E), kind),
            pltpu.SemaphoreType.DMA((Spread.COPIES,)),
            pltpu.SemaphoreType.DMA((Spread.COPIES,)),
        ]

    def __init__(self, place, rows, scratch, term):
        self.rows, self.term = rows, term
        self.parts, self.exact, self.passed, self.arrived, send, recv = scratch
        left, right = place.neighbour(0, RING - 1), place.neighbour(0, 1)
        parts, passed, arrived = self.parts, self.passed, self.arrived
        pairs = (
            (parts.at[2, 0], passed.at[0], left),
            (parts.at[2, 1], passed.at[1], right),
            (parts.at[3, 1], arrived.at[0, 1], left),
            (parts.at[1, 0], arrived.at[1, 0], right),
            (parts.at[3, 0], arrived.at[0, 0], left),
            (parts.at[1, 1], arrived.at[1, 1], right),
        )
        self.copies = [
            remote_copy(src, dst, send.at[at], recv.at[at], device)
            for at, (src, dst, device) in enumerate(pairs)
        ]

    def begin(self):
        for at, (m, i) in enumerate(((2, 0), (2, 1), (3, 1), (1, 0))):
            for r in range(self.rows):
                self.parts[m, i, r] = self.term(m, i, r).astype(self.parts.dtype)
            self.copies[at].start()

    def pass_on(self):
        for at, (m, i) in enumerate(((3, 0), (1, 1))):
            for r in range(self.rows):
                self.exact[at, r] = self.term(m, i, r).astype(F32)
        for at, (m, i) in enumerate(((3, 0), (1, 1))):
            self.copies[at].wait_recv()
            for r in range(self.rows):
                self.parts[m, i, r] = (
                    self.exact[at, r] + self.passed[i, r].astype(F32)
                ).astype(self.parts.dtype)
            self.copies[4 + at].start()

    def arrive(self):
        for copy in self.copies[2:]:
            copy.wait_recv()

    def result(self, i, r):
        return (
            self.term(0, i, r).astype(F32)
            + self.arrived[0, i, r].astype(F32)
            + self.arrived[1, i, r].astype(F32)
        )

    def finish(self):
        for copy in self.copies:
            copy.wait_send()


class SplitSpread(Spread):
    LEGS = 4

    @staticmethod
    def scratch(rows, kind):
        each = rows // 2
        return [
            pltpu.VMEM((RING, HALF, rows, E, E), kind),
            pltpu.VMEM((2, rows, E, E), F32),
            pltpu.VMEM((HALF, rows, E, E), kind),
            pltpu.VMEM((2, 2, HALF, each, E, E), kind),
            pltpu.VMEM((HALF, each, E, E), F32),
            pltpu.VMEM((HALF, each, E, E), F32),
            pltpu.SemaphoreType.DMA((3,)),
            pltpu.SemaphoreType.DMA((3,)),
            pltpu.SemaphoreType.DMA((SplitSpread.LEGS, 2)),
            pltpu.SemaphoreType.DMA((SplitSpread.LEGS, 2)),
        ]

    def __init__(self, place, rows, scratch, term):
        self.rows, self.term, self.place = rows, term, place
        self.parts, self.exact, self.passed, self.arrived, self.mail, self.mailed = scratch[:6]
        send, recv, leg_send, leg_recv = scratch[6:]
        left, right = place.neighbour(0, RING - 1), place.neighbour(0, 1)
        each = rows // 2
        self.far = [
            remote_copy(self.parts.at[2, 0], self.passed.at[0], send.at[0], recv.at[0], left),
            remote_copy(self.parts.at[2, 1], self.passed.at[1], send.at[1], recv.at[1], right),
        ]
        self.swap = remote_copy(self.mail, self.mailed, send.at[2], recv.at[2], place.partner())
        self.legs, self.awaited = [], []
        for leg, (m, i, side) in enumerate(((3, 1, 0), (1, 0, 1), (3, 0, 0), (1, 1, 1))):
            chip = place.chip_at(0, m)
            self.legs.append([])
            for cd in range(2):
                src = self.parts.at[m, i, pl.ds(each * cd, each)]
                self.legs[-1].append(
                    remote_copy(
                        src,
                        self.arrived.at[place.core, side, i],
                        leg_send.at[leg, cd],
                        leg_recv.at[leg, place.core],
                        (chip + cd, place.head),
                    )
                )
                self.awaited.append(
                    remote_copy(
                        src,
                        self.arrived.at[cd, side, i],
                        leg_send.at[leg, cd],
                        leg_recv.at[leg, cd],
                        (chip + cd, place.head),
                    )
                )

    def begin(self):
        each = self.rows // 2
        for at, (m, i) in enumerate(((2, 0), (2, 1), (3, 1), (1, 0))):
            for r in range(self.rows):
                self.parts[m, i, r] = self.term(m, i, *divmod(r, each)).astype(self.parts.dtype)
            for copy in self.far[at : at + 1] if at < 2 else self.legs[at - 2]:
                copy.start()
        for i in range(HALF):
            for r in range(each):
                self.mail[i, r] = self.term(0, i, 1 - self.place.core, r)
        self.swap.start()

    def pass_on(self):
        each = self.rows // 2
        for at, (m, i) in enumerate(((3, 0), (1, 1))):
            for r in range(self.rows):
                self.exact[at, r] = self.term(m, i, *divmod(r, each))
        for at, (m, i) in enumerate(((3, 0), (1, 1))):
            self.far[at].wait_recv()
            for r in range(self.rows):
                self.parts[m, i, r] = (
                    self.exact[at, r] + self.passed[i, r].astype(F32)
                ).astype(self.parts.dtype)
            for copy in self.legs[2 + at]:
                copy.start()

    def arrive(self):
        self.swap.wait_recv()
        for copy in self.awaited:
            copy.wait_recv()

    def result(self, i, r, own):
        core = self.place.core
        side = core if own else 1 - core
        base = self.term(0, i, core, r) if own else self.mailed[i, r]
        return base + self.arrived[side, 0, i, r].astype(F32) + self.arrived[side, 1, i, r].astype(F32)

    def finish(self):
        for copy in self.far + [self.swap] + self.legs[0] + self.legs[1] + self.legs[2] + self.legs[3]:
            copy.wait_send()


class Gather:
    COPIES = 6

    def __init__(self, place, block, send, recv):
        left, right = place.neighbour(RING - 1, 0), place.neighbour(1, 0)
        pairs = (
            (block(0, 0), block(1, 0), left),
            (block(0, 1), block(3, 1), right),
            (block(0, 1), block(1, 1), left),
            (block(0, 0), block(3, 0), right),
            (block(1, 0), block(2, 0), left),
            (block(3, 1), block(2, 1), right),
        )
        self.copies = [
            remote_copy(src, dst, send.at[at], recv.at[at], device)
            for at, (src, dst, device) in enumerate(pairs)
        ]

    def begin(self):
        for copy in self.copies[:4]:
            copy.start()

    def pass_on(self):
        for at in range(2):
            self.copies[at].wait_recv()
            self.copies[4 + at].start()

    def arrive(self):
        for copy in self.copies[2:]:
            copy.wait_recv()
        for copy in self.copies:
            copy.wait_send()


class CrossGather:
    def __init__(self, place, mail, slot, block, scratch):
        send, recv, on_send, on_recv = scratch
        core = place.core
        hops = ((0, RING - 1, 1), (1, 1, 3), (1, RING - 1, 1), (0, 1, 3))
        self.near, self.cross, self.awaited = [], [], []
        for at, (i, move, k) in enumerate(hops):
            near = place.neighbour(move, 0)
            other = (place.chip_at(0, move) + 1 - core, place.head)
            self.near.append(
                remote_copy(
                    slot(0, i, core), slot(k, i, core), send.at[at, 0], recv.at[at, core], near
                )
            )
            self.cross.append(
                remote_copy(mail(i), slot(k, i, core), send.at[at, 1], recv.at[at, core], other)
            )
            self.awaited.append(
                [
                    remote_copy(
                        slot(0, i, cd), slot(k, i, cd), send.at[at, 0], recv.at[at, cd], near
                    )
                    for cd in range(2)
                ]
            )
        self.onward = [
            remote_copy(
                block(1, 0),
                block(2, 0),
                on_send.at[0],
                on_recv.at[0],
                place.neighbour(RING - 1, 0),
            ),
            remote_copy(
                block(3, 1), block(2, 1), on_send.at[1], on_recv.at[1], place.neighbour(1, 0)
            ),
        ]

    def begin(self, copies):
        for copy in copies:
            copy.start()

    def take(self, at):
        for copy in self.awaited[at]:
            copy.wait_recv()

    def pass_on(self):
        for at in range(2):
            self.take(at)
            self.onward[at].start()

    def arrive(self):
        self.take(2)
        self.take(3)
        for copy in self.onward:
            copy.wait_recv()
        for copy in self.near + self.cross + self.onward:
            copy.wait_send()


def remote_copy(src, dst, send, recv, device):
    return pltpu.make_async_remote_copy(
        src_ref=src,
        dst_ref=dst,
        send_sem=send,
        recv_sem=recv,
        device_id=device,
        device_id_type=MESH,
    )


def flag(condition):
    return jnp.where(condition, 1.0, 0.0).astype(F32)


def lanes(head):
    return pl.ds(pl.multiple_of(head * E, E), E)


def main_kernel(
    ends_ref,
    cand_ref,
    lens_ref,
    ranks_ref,
    readout_ref,
    pq_hbm,
    pk_hbm,
    pv_hbm,
    pg_hbm,
    cq_hbm,
    ck_hbm,
    cv_hbm,
    dq_hbm,
    dkp_hbm,
    dvp_hbm,
    cdq_hbm,
    cdk_hbm,
    cdv_hbm,
    right_ref,
    loss_ref,
    pq,
    pk,
    pv,
    pg,
    cq,
    ck,
    cv,
    masks,
    dq_acc,
    dkp,
    dvp,
    dq_out,
    cdq,
    cdk,
    cdv,
    own,
    theirs,
    mail,
    qg_own,
    qg_theirs,
    qg_mail,
    states,
    carry_mail,
    carry_in,
    carry,
    chip_carry,
    later_mail,
    later_in,
    attn_ref,
    outs_ref,
    dout_ref,
    grads_mail,
    mine_ref,
    heads_ref,
    total_ref,
    scores_ref,
    gathered,
    gathered_wide,
    gathered_qg,
    gathered_grads,
    table_ref,
    firsts_ref,
    seconds_ref,
    lasts_ref,
    dk_out,
    dv_out,
    in_sem,
    out_sem,
    swap_send,
    swap_recv,
    ring_send,
    ring_recv,
    y_send,
    y_recv,
    s_send,
    s_recv,
    cross_send,
    cross_recv,
    onward_send,
    onward_recv,
    *spread_scratch,
):
    place = Place()
    core = place.core
    slabs = lax.axis_size("seq")
    planes = lax.axis_size("head")
    width = pq.shape[0]
    cand_width = cq.shape[0]
    scaling = 1.0 / math.sqrt(E * width)
    barrier = pltpu.get_barrier_semaphore()

    def other_slab(at):
        return (place.seq + at) % slabs, place.head

    def hello(at, held):
        pl.semaphore_signal(barrier, inc=1, device_id=other_slab(at), device_id_type=MESH)
        return held

    loads = [
        pltpu.make_async_copy(src, dst, in_sem.at[at])
        for at, (src, dst) in enumerate(
            (
                (pk_hbm, pk),
                (pv_hbm, pv),
                (pg_hbm, pg),
                (pq_hbm, pq),
                (cq_hbm, cq),
                (ck_hbm, ck),
                (cv_hbm, cv),
            )
        )
    ]
    loads[0].start()
    loads[1].start()
    lax.fori_loop(slabs // 2, slabs, hello, 0)
    lax.fori_loop(1, slabs // 2, hello, 0)
    planes_other = [(place.seq, (place.head + at) % planes) for at in range(1, planes)]
    for device in planes_other:
        pl.semaphore_signal(barrier, inc=1, device_id=device, device_id_type=MESH)

    def store(at, src, dst):
        copy = pltpu.make_async_copy(src, dst, out_sem.at[at])
        copy.start()
        return copy

    def swap(at, src, dst):
        return remote_copy(src, dst, swap_send.at[at], swap_recv.at[at], place.partner())

    chip = place.chip_at(0, 0)
    seam_at = (chip + 1) * width
    first0, last0, first1, last1 = counts_of(
        ends_ref, (chip * width, seam_at - 1, seam_at, seam_at + width - 1)
    )
    end0, end1 = local_ends(
        jnp.where(core == 0, first0, first1), ends_ref, place.seq, width
    )
    spot = lax.broadcasted_iota(jnp.int32, (width, E), 0)
    masks[0] = flag(spot < end0).astype(BF)
    masks[1] = flag(jnp.logical_and(spot >= end0, spot < end1)).astype(BF)
    masks[2] = flag(spot >= end1).astype(BF)

    def piece_sums(head):
        v = pv[:, lanes(head)]
        split = jnp.concatenate([v * masks[j] for j in range(PIECES)], axis=1)
        return dot_tn(pk[:, lanes(head)], split)

    loads[0].wait()
    loads[1].wait()
    for load in loads[2:]:
        load.start()
    pieces_swaps = []
    for i in range(HALF):
        sums = piece_sums(HALF * (1 - core) + i)
        for j in range(PIECES):
            mail[i, j] = sums[:, j * E : (j + 1) * E]
        pieces_swaps.append(swap(6 * i, mail.at[i], theirs.at[i, pl.ds(0, PIECES)]))
    pl.semaphore_wait(barrier, slabs - 1 + planes - 1)
    for copy in pieces_swaps:
        copy.start()
    for i in range(HALF):
        sums = piece_sums(HALF * core + i)
        for j in range(PIECES):
            own[j, i] = sums[:, j * E : (j + 1) * E]
        own[PIECES, i] = jnp.zeros((E, E), F32)
        theirs[i, PIECES] = jnp.zeros((E, E), F32)
        for k in range(RING):
            gathered[k, i, CHIP_ENDS - 1] = jnp.zeros((E, E), BF)
            gathered_wide[k, i, 2] = jnp.zeros((E, E), F32)
            gathered_grads[k, i, NONE] = jnp.zeros((E, E), BF)

    off = jnp.clip(first1 - first0, 0, PIECES - 1)
    off_own, off_theirs = off * core, off * (1 - core)

    def slot_in(j, count):
        return jnp.where(jnp.logical_and(j >= 0, j < count), j, count)

    def chip_row(i, j):
        at_own, at_theirs = slot_in(j - off_own, PIECES), slot_in(j - off_theirs, PIECES)
        return own[at_own, i] + theirs[i, at_theirs]

    tail0 = jnp.where(last0 == last1, slot_in(last0 - first0, PIECES), PIECES)
    tail1 = slot_in(last1 - first1, PIECES)
    tail_own = jnp.where(core == 0, tail0, tail1)
    tail_theirs = jnp.where(core == 0, tail1, tail0)
    wide_ring = Gather(
        place,
        lambda k, i: gathered_wide.at[k, i, pl.ds(0, 2)],
        ring_send.at[0],
        ring_recv.at[0],
    )
    ends_ring = Gather(
        place,
        lambda k, i: gathered.at[k, i, pl.ds(0, CHIP_ENDS - 1)],
        ring_send.at[1],
        ring_recv.at[1],
    )
    for copy in pieces_swaps:
        copy.wait()
    for i in range(HALF):
        gathered_wide[0, i, 0] = chip_row(i, 0)
        gathered_wide[0, i, 1] = own[tail_own, i] + theirs[i, tail_theirs]
    wide_ring.begin()
    for i in range(HALF):
        for j in range(1, CHIP_ENDS):
            gathered[0, i, j - 1] = chip_row(i, j).astype(BF)
    ends_ring.begin()

    def count_chip(at, held):
        start = at * 2 * width
        firsts_ref[at], seconds_ref[at], lasts_ref[at] = counts_of(
            ends_ref, (start, start + width, start + 2 * width - 1)
        )
        return held

    lax.fori_loop(0, slabs // 2, count_chip, 0)

    def first_of(seq):
        return firsts_ref[seq // 2]

    def last_of(seq):
        return lasts_ref[seq // 2]

    def segment_of(at):
        return (at >= end0).astype(jnp.int32) + (at >= end1).astype(jnp.int32)

    def prompt_task(at, low, high):
        rows = slice(at * CHUNK, (at + 1) * CHUNK)
        span = (at + 1) * CHUNK
        i = lax.broadcasted_iota(jnp.int32, (CHUNK, 1), 0) + at * CHUNK
        j = lax.broadcasted_iota(jnp.int32, (1, span), 1)
        same = jnp.logical_and(segment_of(i) == segment_of(j), j <= i)

        def one(h, held):
            cols = lanes(h)
            q, g = pq[rows, cols], pg[rows, cols]
            attn = jnp.where(same, dot_nt(q, pk[:span, cols]), 0.0).astype(BF)
            weights = jnp.where(same, dot_nt(g, pv[:span, cols]), 0.0).astype(BF)
            dq_acc[rows, cols] = dot_nn(weights, pk[:span, cols])
            dk = scaling * dot_tn(weights, q)
            dv = scaling * dot_tn(attn, g)
            if span == width:
                dkp[:, cols] = dk
                dvp[:, cols] = dv
            else:
                dkp[:span, cols] += dk
                dvp[:span, cols] += dv
            return held

        lax.fori_loop(low, high, one, 0)

    len0 = lens_ref[0, 0]
    len1 = lens_ref[0, 1]
    in_second = lax.broadcasted_iota(jnp.int32, (cand_width, 1), 0) >= len0

    def same_cand():
        i = lax.broadcasted_iota(jnp.int32, (cand_width, 1), 0)
        j = lax.broadcasted_iota(jnp.int32, (1, cand_width), 1)
        return jnp.logical_and(j <= i, (i >= len0).astype(jnp.int32) == (j >= len0).astype(jnp.int32))

    def cand_near(low, high):
        if low == 0:
            for load in loads[4:]:
                load.wait()

        def one(h, held):
            cols = lanes(h)
            attn = jnp.where(same_cand(), dot_nt(cq[:, cols], ck[:, cols]), 0.0).astype(BF)
            attn_ref[h] = attn
            outs_ref[h] = dot_nn(attn, cv[:, cols])
            return held

        lax.fori_loop(low, high, one, 0)

    def cand_backward(low, high):
        def one(h, held):
            cols = lanes(h)
            dout = dout_ref[h]
            weights = jnp.where(same_cand(), dot_nt(dout, cv[:, cols]), 0.0).astype(BF)
            far = jnp.where(in_second, dot_nt(dout, states[1, h]), dot_nt(dout, states[0, h]))
            cdq[:, cols] = (scaling * (dot_nn(weights, ck[:, cols]) + far)).astype(BF)
            cdk[:, cols] = (scaling * dot_tn(weights, cq[:, cols])).astype(BF)
            cdv[:, cols] = (scaling * dot_tn(attn_ref[h], dout)).astype(BF)
            return held

        lax.fori_loop(low, high, one, 0)

    def dq_finish():
        def one(h, held):
            cols = lanes(h)
            far = dot_nt(pg[:, cols], carry[h])
            inside = lax.broadcasted_iota(jnp.int32, (width, 1), 0) < end0
            dq_out[:, cols] = (scaling * (dq_acc[:, cols] + jnp.where(inside, far, 0.0))).astype(BF)
            return held

        lax.fori_loop(0, LOCAL_HEADS, one, 0)

    loads[2].wait()
    loads[3].wait()

    def qg_sum(head):
        return scaling * dot_tn(pq[:, lanes(head)], pg[:, lanes(head)] * masks[0])

    for i in range(HALF):
        qg_mail[i] = qg_sum(HALF * (1 - core) + i)
    qg_swap = swap(1, qg_mail, qg_theirs)
    qg_swap.start()
    for i in range(HALF):
        qg_own[i] = qg_sum(HALF * core + i)
    wide_ring.pass_on()
    ends_ring.pass_on()
    prompt_task(3, 0, 3)
    whole = flag(off == 0)

    def carry_term(m, i):
        dest = place.chip_at(0, m)
        total = None
        for k in range(RING):
            src = place.chip_at(k, 0)
            same = jnp.logical_and(last_of(src) == first_of(dest), src < dest)
            term = gathered_wide[k, i, jnp.where(same, 1, 2)]
            total = term if total is None else total + term
        return total

    def memory_term(m, i, r):
        if r == 0:
            return carry_term(m, i)
        dest = place.chip_at(0, m)
        total = None
        for k in range(RING):
            src = place.chip_at(k, 0)
            same = jnp.logical_and(first_of(src) == last_of(dest), src > dest)
            term = flag(same) * gathered_qg[k, i]
            total = term if total is None else total + term
        return total

    def state_term(m, i, cd, r):
        wanted = cand_ref[2 * (place.chip_at(0, m) + cd) + r]
        source = jnp.clip((ends_ref[wanted] - 1) // (2 * width), 0, slabs // 2 - 1)
        src_z, src_x = source // RING, source % RING
        src_a = jnp.where(core == 0, src_z, src_x)
        src_b = jnp.where(core == 0, src_x, src_z)
        k_end = (src_a - place.pos_a + RING) % RING
        row = wanted - first_of(2 * source)
        inner = jnp.logical_and(src_b == place.pos_b, row > 0)
        total = gathered[k_end, i, jnp.where(inner, jnp.minimum(row - 1, CHIP_ENDS - 2), CHIP_ENDS - 1)].astype(F32)
        for k in range(RING):
            src = place.chip_at(k, 0)
            opens = jnp.logical_and(src < 2 * source, last_of(src) == wanted)
            ends = jnp.logical_and(src == 2 * source, row == 0)
            total = total + gathered_wide[k, i, jnp.where(opens, 1, jnp.where(ends, 0, 2))]
        return total

    def grad_term(m, i, cd, j):
        at = place.chip_at(0, m) // 2
        wanted = jnp.where(cd == 0, firsts_ref[at], seconds_ref[at]) + j
        total = None
        for k in range(RING):
            src = 2 * place.chip_at(k, 0)
            is0, is1, is2, is3 = [cand_ref[src + c] == wanted for c in range(4)]
            slot0 = jnp.where(is0, jnp.where(is1, SUM01, 0), jnp.where(is1, 1, NONE))
            slot1 = jnp.where(is2, jnp.where(is3, SUM23, 2), jnp.where(is3, 3, NONE))
            term = gathered_grads[k, i, slot0].astype(F32) + gathered_grads[k, i, slot1].astype(F32)
            total = term if total is None else total + term
        return total

    to_states = SplitSpread(place, 4, spread_scratch[:10], state_term)
    to_memory = Spread(place, 2, spread_scratch[10:16], memory_term)
    to_grads = SplitSpread(place, 2 * PIECES, spread_scratch[16:], grad_term)

    qg_swap.wait()
    own_scale = jnp.where(core == 0, 1.0, whole)
    their_scale = jnp.where(core == 0, whole, 1.0)
    for i in range(HALF):
        gathered_qg[0, i] = own_scale * qg_own[i] + their_scale * qg_theirs[i]
    qg_ring = Gather(place, lambda k, i: gathered_qg.at[k, i], ring_send.at[2], ring_recv.at[2])
    wide_ring.arrive()
    ends_ring.arrive()
    qg_ring.begin()
    to_states.begin()
    cand_near(0, 2)
    to_states.pass_on()
    qg_ring.pass_on()
    cand_near(2, 4)
    prompt_task(3, 3, 4)
    to_states.arrive()
    for i in range(HALF):
        for r in range(2):
            states[r, HALF * core + i] = to_states.result(i, r, True).astype(BF)
            states[r, HALF * (1 - core) + i] = to_states.result(i, r, False).astype(BF)

    sum_all = jnp.zeros((1, E), F32)
    sum_second = jnp.zeros((1, E), F32)
    for h in range(LOCAL_HEADS):
        cols = slice(h * E, (h + 1) * E)
        far = jnp.where(
            in_second, dot_nn(cq[:, cols], states[1, h]), dot_nn(cq[:, cols], states[0, h])
        )
        out = scaling * (outs_ref[h] + far)
        outs_ref[h] = out
        part = out / (1.0 + jnp.exp(-out)) * readout_ref[:, cols]
        sum_all = sum_all + jnp.sum(part, axis=0, keepdims=True)
        sum_second = sum_second + jnp.sum(jnp.where(in_second, part, 0.0), axis=0, keepdims=True)
    second = jnp.sum(sum_second, axis=1, keepdims=True)
    first = jnp.sum(sum_all - sum_second, axis=1, keepdims=True)
    lane = lax.broadcasted_iota(jnp.int32, (1, E), 1)
    mine_ref[...] = jnp.where(
        lane == 0,
        first / len0.astype(F32),
        jnp.where(lane == 1, second / len1.astype(F32), 0.0),
    )
    to_planes = [
        remote_copy(mine_ref, heads_ref.at[place.head], y_send.at[at], y_recv.at[at], device)
        for at, device in enumerate(planes_other)
    ]
    for copy in to_planes:
        copy.start()
    heads_ref[place.head] = mine_ref[...]
    qg_ring.arrive()
    to_memory.begin()
    prompt_task(2, 0, 2)
    for copy in to_planes:
        copy.wait()
    total = heads_ref[0]
    for at in range(1, planes):
        total = total + heads_ref[at]
    total_ref[...] = total

    def score_copy(at):
        return remote_copy(
            total_ref, scores_ref.at[place.seq], s_send.at[at], s_recv.at[at], other_slab(at)
        )

    def tell(at, held):
        score_copy(at).start()
        return held

    def told(at, held):
        score_copy(at).wait()
        return held

    def build_table():
        rows = lax.broadcasted_iota(jnp.int32, (slabs, E), 0)

        def one(at, held):
            here = rows == at
            values = (
                cand_ref[2 * at],
                cand_ref[2 * at + 1],
                ranks_ref[2 * at],
                ranks_ref[2 * at + 1],
            )
            return tuple(jnp.where(here, value, old) for value, old in zip(values, held))

        blank = jnp.zeros((slabs, E), jnp.int32)
        for at, plane in enumerate(lax.fori_loop(0, slabs, one, (blank,) * 4)):
            table_ref[at] = plane

    lax.fori_loop(slabs // 2, slabs, tell, 0)
    lax.fori_loop(1, slabs // 2, tell, 0)
    scores_ref[place.seq] = total
    build_table()
    to_memory.pass_on()
    prompt_task(2, 2, 4)
    lax.fori_loop(1, slabs, told, 0)

    raw = scores_ref[...].reshape(slabs, E)
    prompts = lax.broadcasted_iota(jnp.int32, (slabs, E), 1)
    tanh_raw = jnp.tanh(raw)
    squashed = 3.0 * tanh_raw
    exp_scores = jnp.exp(squashed)
    hot = [(table_ref[j] == prompts).astype(F32) for j in range(2)]
    weight = [jnp.exp(-table_ref[2 + j].astype(F32)) for j in range(2)]
    group_exp = jnp.sum(
        hot[0] * exp_scores[:, 0:1] + hot[1] * exp_scores[:, 1:2], axis=0, keepdims=True
    )
    group_weight = jnp.sum(hot[0] * weight[0] + hot[1] * weight[1], axis=0, keepdims=True)
    own_row = lax.broadcasted_iota(jnp.int32, (slabs, 1), 0) == place.seq
    loss = jnp.zeros((1, 1), F32)
    coefs = []
    for j in range(2):
        denom = jnp.sum(hot[j] * group_exp, axis=1, keepdims=True)
        target = weight[j][:, 0:1] / jnp.sum(hot[j] * group_weight, axis=1, keepdims=True)
        score = squashed[:, j : j + 1]
        loss = loss + jnp.sum(target * (score - jnp.log(denom)), axis=0, keepdims=True)
        tanh_j = tanh_raw[:, j : j + 1]
        grad = (
            GRAD_SCALE
            / slabs
            * (exp_scores[:, j : j + 1] / denom - target)
            * 3.0
            * (1.0 - tanh_j * tanh_j)
        )
        coefs.append(jnp.sum(jnp.where(own_row, grad, 0.0), axis=0, keepdims=True))
    loss_ref[...] = -loss / slabs
    coef = jnp.where(in_second, coefs[1] / len1.astype(F32), coefs[0] / len0.astype(F32))

    def grad_sums(h):
        out = outs_ref[h]
        sigma = 1.0 / (1.0 + jnp.exp(-out))
        slope = coef * readout_ref[:, lanes(h)] * sigma * (1.0 + out * (1.0 - sigma))
        dout_ref[h] = slope.astype(BF)
        split = jnp.concatenate(
            [
                jnp.where(in_second, 0.0, slope).astype(BF),
                jnp.where(in_second, slope, 0.0).astype(BF),
            ],
            axis=1,
        )
        return scaling * dot_tn(cq[:, lanes(h)], split)

    for i in range(HALF):
        sums = grad_sums(HALF * (1 - core) + i)
        for r in range(2):
            grads_mail[i, r] = sums[:, r * E : (r + 1) * E].astype(BF)
    own_slots = pl.ds(2 * core, 2)
    grads_swap = swap(3, grads_mail, gathered_grads.at[0, :, own_slots])
    grads_ring = CrossGather(
        place,
        lambda i: grads_mail.at[i],
        lambda k, i, cd: gathered_grads.at[k, i, pl.ds(2 * cd, 2)],
        lambda k, i: gathered_grads.at[k, i, pl.ds(0, 4)],
        (cross_send, cross_recv, onward_send, onward_recv),
    )
    grads_ring.begin(grads_ring.cross)
    grads_swap.start()
    for i in range(HALF):
        sums = grad_sums(HALF * core + i)
        for r in range(2):
            gathered_grads[0, i, 2 * core + r] = sums[:, r * E : (r + 1) * E].astype(BF)
    grads_ring.begin(grads_ring.near)
    grads_swap.wait()

    to_memory.arrive()
    seam = slot_in(off, PIECES)

    def carry_row(i, at_core):
        before = jnp.where(core == 0, own[seam, i], theirs[i, seam])
        is_second = flag(at_core == 1)
        keep = jnp.where(at_core == 0, 1.0, whole)
        return (keep * chip_carry[i] + is_second * before).astype(BF)

    def later_row(i, at_core):
        chip_later = to_memory.result(i, 1)
        second_qg = jnp.where(core == 0, qg_theirs[i], qg_own[i])
        inner = flag(first1 == last0) * second_qg + flag(last1 == last0) * chip_later
        return jnp.where(at_core == 0, inner, chip_later)

    for i in range(HALF):
        later_mail[i] = later_row(i, 1 - core)
        chip_carry[i] = to_memory.result(i, 0)
        carry_mail[i] = carry_row(i, 1 - core)
    carry_swap = swap(4, carry_mail, carry_in)
    later_swap = swap(5, later_mail, later_in)
    carry_swap.start()
    later_swap.start()
    for i in range(HALF):
        carry[HALF * core + i] = carry_row(i, core)
    cand_backward(0, 2)
    grads_ring.pass_on()
    cand_backward(2, 4)
    prompt_task(1, 0, 2)
    outputs = [store(0, cdq, cdq_hbm), store(1, cdk, cdk_hbm), store(2, cdv, cdv_hbm)]
    carry_swap.wait()
    later_swap.wait()
    for i in range(HALF):
        carry[HALF * (1 - core) + i] = carry_in[i]
    grads_ring.arrive()
    for k in range(RING):
        for i in range(HALF):
            for target, source in ((SUM01, 0), (SUM23, 2)):
                gathered_grads[k, i, target] = (
                    gathered_grads[k, i, source].astype(F32)
                    + gathered_grads[k, i, source + 1].astype(F32)
                ).astype(BF)
    to_grads.begin()
    prompt_task(1, 2, 4)
    to_grads.pass_on()
    prompt_task(0, 0, 4)
    dk_out[...] = dkp[...].astype(BF)
    dv_out[...] = dvp[...].astype(BF)
    outputs += [store(3, dk_out, dkp_hbm), store(4, dv_out, dvp_hbm)]
    dq_finish()
    outputs.append(store(5, dq_out, dq_hbm))
    to_grads.arrive()
    into = jnp.where(core == 0, last0 - first0, last1 - first1)
    for i in range(HALF):
        for side, own_side in ((core, True), (1 - core, False)):
            later = later_row(i, core) if own_side else later_in[i]
            for j in range(PIECES):
                right_ref[j, HALF * side + i] = (
                    to_grads.result(i, j, own_side) + flag(into == j) * later
                ).astype(BF)
    for spread in (to_states, to_memory, to_grads):
        spread.finish()
    for copy in outputs:
        copy.wait()


def last_kernel(
    ends_ref,
    k_ref,
    v_ref,
    dkp_ref,
    dvp_ref,
    right_ref,
    dq_in,
    cdq_in,
    cdk_in,
    cdv_in,
    dq_ref,
    dk_ref,
    dv_ref,
    cdq_ref,
    cdk_ref,
    cdv_ref,
):
    width = k_ref.shape[0]
    slab = lax.axis_index("seq")
    first = counts_of(ends_ref, (slab * width,))[0]
    end0, end1 = local_ends(first, ends_ref, slab, width)
    spot = lax.broadcasted_iota(jnp.int32, (width, 1), 0)
    k, v = k_ref[...], v_ref[...]
    rows = [right_ref[j, 0] for j in range(PIECES)]
    dk = dot_nt(v, jnp.concatenate(rows, axis=0))
    dv = dot_nn(k, jnp.concatenate(rows, axis=1))
    for out, part, wide in ((dk_ref, dkp_ref, dk), (dv_ref, dvp_ref, dv)):
        far = [wide[:, j * E : (j + 1) * E] for j in range(PIECES)]
        chosen = jnp.where(spot < end0, far[0], jnp.where(spot < end1, far[1], far[2]))
        out[...] = (part[...].astype(F32) + chosen).astype(BF)
    dq_ref[...] = dq_in[...]
    cdq_ref[...] = cdq_in[...]
    cdk_ref[...] = cdk_in[...]
    cdv_ref[...] = cdv_in[...]


def per_device(
    prompt_q,
    prompt_k,
    prompt_v,
    prompt_grad,
    cand_q,
    cand_k,
    cand_v,
    readout,
    prompt_ends,
    cand_lengths,
    cand_prompt,
    cand_ranks,
):
    slabs = lax.axis_size("seq")
    width = prompt_q.shape[0]
    cand_width = cand_q.shape[0]
    flat = prompt_q.shape[1]
    any_spec = pl.BlockSpec(memory_space=pl.ANY)
    prompt_shape = jax.ShapeDtypeStruct((width, flat), BF)
    cand_shape = jax.ShapeDtypeStruct((cand_width, flat), BF)
    prompt_buf = pltpu.VMEM((width, flat), BF)
    prompt_acc = pltpu.VMEM((width, flat), F32)
    cand_buf = pltpu.VMEM((cand_width, flat), BF)
    half_rows = lambda *lead, kind=BF: pltpu.VMEM(lead + (E, E), kind)
    dma = pltpu.SemaphoreType.DMA
    dq_part, dk_part, dv_part, cand_dq, cand_dk, cand_dv, right, loss = pl.pallas_call(
        main_kernel,
        out_shape=(
            prompt_shape,
            prompt_shape,
            prompt_shape,
            cand_shape,
            cand_shape,
            cand_shape,
            jax.ShapeDtypeStruct((PIECES, LOCAL_HEADS, E, E), BF),
            jax.ShapeDtypeStruct((1, 1), F32),
        ),
        in_specs=[SMEM_SPEC] * 4 + [VMEM_SPEC] + [any_spec] * 7,
        out_specs=[any_spec] * 6 + [VMEM_SPEC] * 2,
        scratch_shapes=[prompt_buf] * 4
        + [cand_buf] * 3
        + [pltpu.VMEM((PIECES, width, E), BF)]
        + [prompt_acc] * 3
        + [prompt_buf]
        + [cand_buf] * 3
        + [
            half_rows(PIECES + 1, HALF, kind=F32),
            half_rows(HALF, PIECES + 1, kind=F32),
            half_rows(HALF, PIECES, kind=F32),
            half_rows(HALF, kind=F32),
            half_rows(HALF, kind=F32),
            half_rows(HALF, kind=F32),
            half_rows(2, LOCAL_HEADS),
            half_rows(HALF),
            half_rows(HALF),
            half_rows(LOCAL_HEADS),
            half_rows(HALF, kind=F32),
            half_rows(HALF, kind=F32),
            half_rows(HALF, kind=F32),
            pltpu.VMEM((LOCAL_HEADS, cand_width, cand_width), BF),
            pltpu.VMEM((LOCAL_HEADS, cand_width, E), F32),
            pltpu.VMEM((LOCAL_HEADS, cand_width, E), BF),
            half_rows(HALF, 2),
            pltpu.VMEM((1, E), F32),
            pltpu.VMEM((4, 1, E), F32),
            pltpu.VMEM((1, E), F32),
            pltpu.VMEM((slabs, 1, E), F32),
            half_rows(RING, HALF, CHIP_ENDS),
            half_rows(RING, HALF, 3, kind=F32),
            half_rows(RING, HALF, kind=F32),
            half_rows(RING, HALF, NONE + 1),
            pltpu.VMEM((4, slabs, E), jnp.int32),
            pltpu.SMEM((slabs // 2,), jnp.int32),
            pltpu.SMEM((slabs // 2,), jnp.int32),
            pltpu.SMEM((slabs // 2,), jnp.int32),
            prompt_buf,
            prompt_buf,
            dma((7,)),
            dma((6,)),
            dma((7,)),
            dma((7,)),
            dma((4, 6)),
            dma((4, 6)),
            dma((3,)),
            dma((3,)),
            dma((slabs,)),
            dma((slabs,)),
            dma((4, 2)),
            dma((4, 2)),
            dma((2,)),
            dma((2,)),
        ]
        + SplitSpread.scratch(4, F32)
        + Spread.scratch(2, F32)
        + SplitSpread.scratch(2 * PIECES, BF),
        compiler_params=pltpu.CompilerParams(
            collective_id=0, has_side_effects=True, vmem_limit_bytes=56 << 20
        ),
        name="exchange",
    )(
        prompt_ends,
        cand_prompt,
        cand_lengths,
        cand_ranks,
        readout.reshape(1, flat),
        prompt_q,
        prompt_k,
        prompt_v,
        prompt_grad,
        cand_q,
        cand_k,
        cand_v,
    )

    prompt_block = pl.BlockSpec((width, E), lambda h: (0, h))
    cand_block = pl.BlockSpec((cand_width, E), lambda h: (0, h))
    prompt_dq, prompt_dk, prompt_dv, cand_dq, cand_dk, cand_dv = pl.pallas_call(
        last_kernel,
        grid=(LOCAL_HEADS,),
        out_shape=(prompt_shape,) * 3 + (cand_shape,) * 3,
        in_specs=[SMEM_SPEC]
        + [prompt_block] * 4
        + [pl.BlockSpec((PIECES, 1, E, E), lambda h: (0, h, 0, 0)), prompt_block]
        + [cand_block] * 3,
        out_specs=(prompt_block,) * 3 + (cand_block,) * 3,
        name="finish",
    )(
        prompt_ends,
        prompt_k,
        prompt_v,
        dk_part,
        dv_part,
        right,
        dq_part,
        cand_dq,
        cand_dk,
        cand_dv,
    )
    return (
        prompt_dq,
        prompt_dk,
        prompt_dv,
        cand_dq,
        cand_dk,
        cand_dv,
        loss.reshape(()),
    )


def solution(mesh):
    both = P("seq", "head")
    return jax.shard_map(
        per_device,
        mesh=mesh,
        in_specs=(
            both,
            both,
            both,
            both,
            both,
            both,
            both,
            P("head"),
            P(),
            P("seq", None),
            P(),
            P(),
        ),
        out_specs=(both, both, both, both, both, both, P()),
        check_vma=False,
    )
```
